256 devices in a mesh: orb: 8 (over z), ri: 8 (over y, core), pair: 4 (over x).
Axes of the slice: x: 4, y: 4, z: 8, core: 2. Of those that a mesh axis runs over, the one named last changes fastest.
Arguments:
- three_center: bfloat16 [4096, 64, 1024], P(('orb', 'ri', 'pair')), may hold values from -0.59765625 to 0.59765625
- block_dest: int32 [4096, 1], P('orb'), may hold values from 0 to 31; in each aligned block of 16 rows (0 to 15, 16 to 31, ...) at most 2 rows name the same one
- block_row: int32 [4096], P('orb'), may hold values from 0 to 7
- block_col: int32 [4096], P('orb'), may hold values from 0 to 7
- occ_density: bfloat16 [256, 256], P('orb'), may hold values from -0.375 to 0.375
- virt_density: bfloat16 [256, 256], P('orb'), may hold values from -0.375 to 0.375
- occ_mask: int32 [8, 8], P('orb'), may hold values 0 or 1
- virt_mask: int32 [8, 8], P('orb'), may hold values 0 or 1
Outputs:
- chi_slabs: float32 [16384, 64], P(('orb', 'ri', 'pair'))
The draws below stay inside these ranges and needn't reach their ends.
Inputs may be any that keep to these rules, and one draw needn't show every extreme that they name: `block_dest`: in the 16 rows of one device, no owner is named by more than 2 rows.
All inputs are finite; a program needn't handle non-finite values. No bound on the sum of `occ_mask` or of `virt_mask` on one device may be relied on, other than what follows from the above.
Results may differ from the reference program's by a relative error of at most 0.0047.
Values may be sent and summed in bfloat16 or wider, within the bound.
No kernel may reach another device: no remote copies, remote signals or barrier semaphores. Data moves between devices by JAX's collectives and lax.ppermute only.
A program may use at most 192 MiB of HBM per device.

```python
import math
import jax
import jax.numpy as jnp
import numpy as np
from jax import lax

BR = 64
BA = 32
KD = 16
AB_DEV = 1
NDEST = 32
CAP = 2
NAB = 8
NAO = 256
NBLK = 4096
N_ORB = 8
N_RI = 8
N_PAIR = 4
DEVICES = 256


def set_ends(result, rng, smallest, largest):
    longest = result.shape.index(max(result.shape))
    spots = []
    for shift in (0, 1):
        where = [jax.random.randint(jax.random.fold_in(rng, axis), (), 0, length) for axis, length in enumerate(result.shape)]
        where[longest] = (where[longest] + shift) % result.shape[longest]
        spots.append(tuple(where))
    return result.at[spots[0]].set(smallest).at[spots[1]].set(largest)


def level_of(rng, dims, shards, least, top_value):
    level, own = 1.0, jax.random.fold_in(rng, 6)
    for dim, blocks in shards:
        heights = jnp.exp(jax.random.uniform(jax.random.fold_in(own, dim), (blocks,), jnp.float32, least / len(shards), top_value / len(shards)))
        level = level * jnp.repeat(heights, dims[dim] // blocks).reshape([-1 if axis == dim else 1 for axis in range(len(dims))])
    return level


def assign_block(key, own, number, rows, count, top, most, skew):
    ranking = jax.random.permutation(key, count)
    crowded, ordinary = load_shares(count, rows * top, most, skew, True), load_shares(count, rows * top, most, skew, False)
    places = jnp.arange(count)

    def named(tallies, offset_by):
        used = int((tallies > 0).sum())
        fixed = max(1, used // 4)
        shifted = fixed + (places - fixed + offset_by * (used - fixed)) % max(1, count - fixed)
        return jnp.zeros((count,), jnp.int32).at[ranking[jnp.where(places < fixed, places, shifted)]].set(jnp.asarray(tallies, jnp.int32))

    tallies = jnp.where(number % 4 == 0, named(crowded, number // 4), named(ordinary, number - number // 4 - 1))
    mixed = jax.random.permutation(jax.random.fold_in(own, 3), count)
    giver, taker = mixed[0:count // 2 * 2:2], mixed[1:count // 2 * 2:2]
    slack = jnp.minimum(tallies[giver] - 1, most - tallies[taker]) // 2
    slack = jnp.where((giver == ranking[0]) | (taker == ranking[0]) | (tallies[taker] == 0), 0, jnp.maximum(slack, 0))
    shifted = jax.random.randint(jax.random.fold_in(own, 4), (count // 2,), 0, 1 << 20) % (slack + 1)
    tallies = tallies.at[giver].add(-shifted).at[taker].add(shifted)
    labels = jnp.searchsorted(jnp.cumsum(tallies), jnp.arange(rows * top), side="right").astype(jnp.int32)
    grid = labels.reshape(top, rows).T
    grid = grid[jax.random.permutation(jax.random.fold_in(own, 1), rows)]
    offset_by = jax.random.randint(jax.random.fold_in(own, 2), (rows, 1), 0, top)
    return jnp.take_along_axis(grid, (jnp.arange(top)[None, :] + offset_by) % top, axis=1)


def load_shares(amount, total, most, slope, full):
    loads = [(1 << 20) // math.isqrt(grade ** slope) + 1 for grade in range(1, amount + 1)]
    largest = most if full else min(most, max(-(-total // amount), total * loads[0] // sum(loads)))
    least = 1 if total - largest >= amount - 1 else 0
    given, spare = [largest] + [least] * (amount - 1), total - largest - least * (amount - 1)
    while spare > 0:
        free = [i for i in range(1, amount) if given[i] < largest] or [i for i in range(1, amount) if given[i] < most]
        whole, budget = sum([loads[i] for i in free]), spare
        for i in free:
            addition = min(most - given[i], max(1, budget * loads[i] // whole), spare)
            given[i] = given[i] + addition
            spare = spare - addition
    return np.array(given)


def centred(rng, shape, scale, bound, split=(), kind=jnp.bfloat16):
    array = scale * jax.random.normal(rng, shape, jnp.float32)
    if split:
        array = array * level_of(rng, shape, split, -0.22, 0.18)
    return jnp.clip(array, -bound, bound).astype(kind)


def setup_inputs(seed: int = 0) -> dict:
    key_list = jax.random.split(jax.random.key(seed), 9)
    three_center = centred(key_list[0], (NBLK, BR, BA * BA), 0.1, 0.59765625, ((0, 256),))
    block_dest_keys = jax.random.split(jax.random.fold_in(key_list[1], 1), NBLK // KD)
    block_dest_turns = jax.random.permutation(jax.random.fold_in(key_list[1], 3), NBLK // KD)
    block_dest = jax.vmap(lambda own, number: assign_block(jax.random.fold_in(key_list[1], 2), own, number, KD, NDEST, 1, CAP, 1))(block_dest_keys, block_dest_turns).reshape((NBLK, 1))
    block_row = set_ends(jax.random.randint(key_list[2], (NBLK,), 0, NAB), jax.random.fold_in(key_list[2], 1), 0, NAB - 1).astype(jnp.int32)
    block_col = set_ends(jax.random.randint(key_list[3], (NBLK,), 0, NAB), jax.random.fold_in(key_list[3], 1), 0, NAB - 1).astype(jnp.int32)
    occ_density = centred(key_list[4], (NAO, NAO), NAO ** -0.5, 0.375, ((0, 8),))
    virt_density = centred(key_list[5], (NAO, NAO), NAO ** -0.5, 0.375, ((0, 8),))
    occ_mask = set_ends((jax.random.randint(key_list[6], (NAB, NAB), 0, 4) < 3).astype(jnp.int32), jax.random.fold_in(key_list[6], 1), 0, 1)
    virt_mask = set_ends((jax.random.randint(key_list[7], (NAB, NAB), 0, 4) < 3).astype(jnp.int32), jax.random.fold_in(key_list[7], 1), 0, 1)
    return {"three_center": three_center, "block_dest": block_dest, "block_row": block_row, "block_col": block_col, "occ_density": occ_density, "virt_density": virt_density, "occ_mask": occ_mask, "virt_mask": virt_mask}


def round_half(values):
    return lax.optimization_barrier(values.astype(jnp.bfloat16)).astype(jnp.float32)


def expand(mask_blocks):
    return jnp.repeat(jnp.repeat(mask_blocks, BA, axis=0), BA, axis=1)


def reference(three_center, block_dest, block_row, block_col, occ_density, virt_density, occ_mask, virt_mask):
    owners = N_RI * N_PAIR
    slot_cap = max(2, (KD + owners - 1) // owners)
    slot_count = owners * slot_cap
    ao_blocks = AB_DEV * N_ORB
    ao_width = ao_blocks * BA
    group_rows = owners * KD
    occ_masked = occ_density * expand(occ_mask).astype(jnp.bfloat16)
    virt_masked = virt_density * expand(virt_mask).astype(jnp.bfloat16)
    occ_rows = occ_masked.astype(jnp.float32).reshape(ao_blocks, BA, ao_width)
    virt_rows = virt_masked.astype(jnp.float32).reshape(ao_blocks, BA, ao_width)

    def one_slab(slab_index):
        group_index = slab_index // owners
        target = slab_index % owners
        first_row = (group_index * group_rows).astype(jnp.int32)
        dest_ids = lax.dynamic_slice_in_dim(block_dest[:, 0], first_row, group_rows)
        row_ids = lax.dynamic_slice_in_dim(block_row, first_row, group_rows)
        col_ids = lax.dynamic_slice_in_dim(block_col, first_row, group_rows)
        matches = dest_ids == target
        picked = jnp.nonzero(matches, size=slot_count, fill_value=0)[0].astype(jnp.int32)
        live_count = jnp.sum(matches.astype(jnp.int32))
        live_weight = (jnp.arange(slot_count, dtype=jnp.int32) < live_count).astype(jnp.float32)
        chosen = jnp.take(three_center, first_row + picked, axis=0).astype(jnp.float32)
        chosen = chosen.reshape(slot_count, BR, BA, BA) * live_weight[:, None, None, None]
        assembled = jnp.zeros((ao_blocks, ao_blocks, BR, BA, BA), jnp.float32)
        assembled = assembled.at[row_ids[picked], col_ids[picked]].add(chosen)
        dense_blocks = round_half(assembled)
        half_done = round_half(jnp.einsum("mul,mnauv->lnav", occ_rows, dense_blocks))
        both_done = round_half(jnp.einsum("lnav,nvs->las", half_done, virt_rows))
        both_five = both_done.reshape(ao_blocks, BA, BR, ao_blocks, BA)
        return jnp.einsum("muanv,mnbuv->ab", both_five, dense_blocks)

    chi_all = lax.map(one_slab, jnp.arange(DEVICES, dtype=jnp.int32))
    return chi_all.reshape(DEVICES * BR, BR)
```

```python
import functools

import jax
import jax.numpy as jnp
from jax import lax
from jax.experimental import pallas as pl
from jax.experimental.pallas import tpu as pltpu
from jax.sharding import PartitionSpec as P

BR = 64
BA = 32
CAP = 2
LANES = 128


def expand(mask_blocks, block_width):
    return jnp.repeat(jnp.repeat(mask_blocks, block_width, axis=0), block_width, axis=1)


def pack_kernel(owners, blocks_dev, me_ref, dest_ref, blocks_ref, out_ref, taken_ref, sem):
    me = me_ref[0]

    def clear(o, _):
        taken_ref[o] = 0
        return 0

    lax.fori_loop(0, owners, clear, 0)

    def send(k, _):
        owner = dest_ref[me * blocks_dev + k]
        rank = taken_ref[owner]
        taken_ref[owner] = rank + 1
        pltpu.make_async_copy(blocks_ref.at[k], out_ref.at[owner * CAP + rank], sem).start()
        return 0

    lax.fori_loop(0, blocks_dev, send, 0)
    pltpu.make_async_copy(blocks_ref, out_ref.at[pl.ds(0, blocks_dev)], sem).wait()


def pack(me, dest, blocks, owners):
    blocks_dev = blocks.shape[0]
    return pl.pallas_call(
        functools.partial(pack_kernel, owners, blocks_dev),
        out_shape=jax.ShapeDtypeStruct((owners * CAP,) + blocks.shape[1:], blocks.dtype),
        in_specs=[
            pl.BlockSpec(memory_space=pltpu.SMEM),
            pl.BlockSpec(memory_space=pltpu.SMEM),
            pl.BlockSpec(memory_space=pl.ANY),
        ],
        out_specs=pl.BlockSpec(memory_space=pl.ANY),
        scratch_shapes=[pltpu.SMEM((owners,), jnp.int32), pltpu.SemaphoreType.DMA],
        name="pack",
    )(me, dest, blocks)


def plan_kernel(owners, blocks_dev, ao_blocks, me_ref, dest_ref, row_ref, col_ref, cell_ref, next_ref, list_ref):
    me = me_ref[0]
    slots = owners * CAP
    cells = ao_blocks * ao_blocks

    def clear(c, _):
        cell_ref[c] = slots
        return 0

    lax.fori_loop(0, cells, clear, 0)

    def source(s, total):
        def block(k, carry):
            rank, total = carry
            index = s * blocks_dev + k
            mine = dest_ref[index] == me

            @pl.when(mine)
            def _():
                slot = s * CAP + rank
                cell = row_ref[index] * ao_blocks + col_ref[index]
                next_ref[slot] = cell_ref[cell]
                cell_ref[cell] = slot
                list_ref[1 + total] = slot

            step = mine.astype(jnp.int32)
            return rank + step, total + step

        return lax.fori_loop(0, blocks_dev, block, (jnp.int32(0), total))[1]

    list_ref[0] = lax.fori_loop(0, owners, source, jnp.int32(0))


def plan(me, dest, row, col, owners, blocks_dev, ao_blocks):
    smem = pl.BlockSpec(memory_space=pltpu.SMEM)
    slots = owners * CAP
    return pl.pallas_call(
        functools.partial(plan_kernel, owners, blocks_dev, ao_blocks),
        out_shape=(
            jax.ShapeDtypeStruct((ao_blocks * ao_blocks,), jnp.int32),
            jax.ShapeDtypeStruct((slots,), jnp.int32),
            jax.ShapeDtypeStruct((slots + 1,), jnp.int32),
        ),
        in_specs=[smem] * 4,
        out_specs=(smem,) * 3,
        name="plan",
    )(me, dest, row, col)


def slab_kernel(
    slots, ao_blocks, cell_ref, next_ref, list_ref, occ_ref, virt_ref, recv_ref, out_ref,
    held, dense, work, total, sem,
):
    count = list_ref[0]
    width = ao_blocks * BA
    per_tile = LANES // BA

    def fetch(i, _):
        slot = list_ref[1 + i]
        pltpu.make_async_copy(recv_ref.at[slot], held.at[slot], sem).start()
        return 0

    lax.fori_loop(0, count, fetch, 0)
    held[slots] = jnp.zeros(held.shape[1:], held.dtype)

    def arrive(i, _):
        pltpu.make_async_copy(recv_ref.at[0], held.at[0], sem).wait()
        return 0

    lax.fori_loop(0, count, arrive, 0)

    def merge(c, _):
        first = cell_ref[c]

        @pl.when(first < slots)
        def _():
            second = next_ref[first]

            @pl.when(second < slots)
            def _():
                total[...] = held[first].astype(jnp.float32)

                def add(slot):
                    total[...] += held[slot].astype(jnp.float32)
                    return next_ref[slot]

                lax.while_loop(lambda slot: slot < slots, add, second)
                held[first] = total[...].astype(held.dtype)

        return 0

    lax.fori_loop(0, ao_blocks * ao_blocks, merge, 0)

    group = lax.broadcasted_iota(jnp.int32, (BR, LANES), 1) // BA
    low_half = group < 2
    even = group % 2 == 0
    tiles = width // LANES

    def place(step, _):
        r = step // tiles
        tile = step % tiles
        lanes = pl.ds(pl.multiple_of(tile * LANES, LANES), LANES)
        sources = [cell_ref[r * ao_blocks + tile * per_tile + j] for j in range(per_tile)]
        for hi in range(BA // per_tile):
            x = [held[s, :, hi * LANES : (hi + 1) * LANES].astype(jnp.float32) for s in sources]
            z = [None] * 4
            for a, b in ((0, 2), (1, 3)):
                z[a] = jnp.where(low_half, x[a], pltpu.roll(x[b], 64, 1))
                z[b] = jnp.where(low_half, pltpu.roll(x[a], 64, 1), x[b])
            y = [None] * 4
            for a, b in ((0, 1), (2, 3)):
                y[a] = jnp.where(even, z[a], pltpu.roll(z[b], 32, 1))
                y[b] = jnp.where(even, pltpu.roll(z[a], 96, 1), z[b])
            for j in range(per_tile):
                mu = r * BA + hi * per_tile + j
                work[tile, pl.ds(pl.multiple_of(mu * BR, BR), BR), :] = y[j]
                dense[mu, :, lanes] = y[j].astype(jnp.bfloat16)
        return 0

    lax.fori_loop(0, ao_blocks * tiles, place, 0)

    occ_t = occ_ref[...]
    virt = virt_ref[...]

    def transform(p, _):
        rows = pl.ds(p, width, stride=BR)
        part = jnp.concatenate([work[t, rows, :] for t in range(tiles)], axis=1).astype(jnp.bfloat16)
        half = jnp.dot(occ_t, part, preferred_element_type=jnp.float32).astype(jnp.bfloat16)
        both = jnp.dot(half, virt, preferred_element_type=jnp.float32)
        for t in range(tiles):
            work[t, rows, :] = both[:, t * LANES : (t + 1) * LANES]
        return 0

    lax.fori_loop(0, BR, transform, 0)

    def contract(i, acc):
        for j in range(4):
            mu = i * 4 + j
            rows = pl.ds(pl.multiple_of(mu * BR, BR), BR)
            both = jnp.concatenate([work[t, rows, :] for t in range(tiles)], axis=1).astype(jnp.bfloat16)
            acc = acc + lax.dot_general(
                both, dense[mu], (((1,), (1,)), ((), ())), preferred_element_type=jnp.float32
            )
        return acc

    out_ref[...] = lax.fori_loop(0, width // 4, contract, jnp.zeros((BR, BR), jnp.float32))


def slab(cell, chain, listed, occ_t, virt, recv, ao_blocks):
    slots = recv.shape[0]
    width = ao_blocks * BA
    smem = pl.BlockSpec(memory_space=pltpu.SMEM)
    vmem = pl.BlockSpec(memory_space=pltpu.VMEM)
    return pl.pallas_call(
        functools.partial(slab_kernel, slots, ao_blocks),
        out_shape=jax.ShapeDtypeStruct((BR, BR), jnp.float32),
        in_specs=[smem, smem, smem, vmem, vmem, pl.BlockSpec(memory_space=pl.ANY)],
        out_specs=vmem,
        scratch_shapes=[
            pltpu.VMEM((slots + 1, BR, BA * BA), jnp.bfloat16),
            pltpu.VMEM((width, BR, width), jnp.bfloat16),
            pltpu.VMEM((width // LANES, width * BR, LANES), jnp.float32),
            pltpu.VMEM((BR, BA * BA), jnp.float32),
            pltpu.SemaphoreType.DMA,
        ],
        compiler_params=pltpu.CompilerParams(vmem_limit_bytes=48 * 1024 * 1024),
        name="slab",
    )(cell, chain, listed, occ_t, virt, recv)


def body(
    three_center, block_dest, block_row, block_col, occ_density, virt_density, occ_mask, virt_mask
):
    owners = lax.axis_size(("ri", "pair"))
    blocks_dev = three_center.shape[0]
    ao_blocks = occ_mask.shape[1]
    width = occ_density.shape[1]
    me = lax.axis_index(("ri", "pair")).astype(jnp.int32).reshape(1)
    dest = block_dest.reshape(-1)
    outgoing = pack(me, dest, three_center, owners)
    incoming = lax.all_to_all(outgoing, ("ri", "pair"), split_axis=0, concat_axis=0, tiled=True)
    local = jnp.concatenate(
        [
            occ_density * expand(occ_mask, BA).astype(jnp.bfloat16),
            virt_density * expand(virt_mask, BA).astype(jnp.bfloat16),
        ],
        axis=1,
    )
    whole = lax.all_gather(local, "orb", axis=0, tiled=True)
    cell, chain, listed = plan(me, dest, block_row, block_col, owners, blocks_dev, ao_blocks)
    return slab(cell, chain, listed, whole[:, :width].T, whole[:, width:], incoming, ao_blocks)


def solution(mesh):
    placed = (
        P(("orb", "ri", "pair"), None, None),
        P("orb", None),
        P("orb"),
        P("orb"),
        P("orb", None),
        P("orb", None),
        P("orb", None),
        P("orb", None),
    )
    return jax.shard_map(
        body, mesh=mesh, in_specs=placed, out_specs=P(("orb", "ri", "pair"), None), check_vma=False
    )
```

```python
import functools

import jax
import jax.numpy as jnp
from jax import lax
from jax.experimental import pallas as pl
from jax.experimental.pallas import tpu as pltpu
from jax.sharding import PartitionSpec as P

BR = 64
BA = 32
CAP = 2
LANES = 128
PITCH = BR + 1


def expand(mask_blocks, block_width):
    return jnp.repeat(jnp.repeat(mask_blocks, block_width, axis=0), block_width, axis=1)


def pack_kernel(owners, blocks_dev, me_ref, dest_ref, blocks_ref, out_ref, taken_ref, sem):
    me = me_ref[0]

    def clear(o, _):
        taken_ref[o] = 0
        return 0

    lax.fori_loop(0, owners, clear, 0)

    def send(k, _):
        owner = dest_ref[me * blocks_dev + k]
        rank = taken_ref[owner]
        taken_ref[owner] = rank + 1
        pltpu.make_async_copy(blocks_ref.at[k], out_ref.at[owner * CAP + rank], sem).start()
        return 0

    lax.fori_loop(0, blocks_dev, send, 0)
    pltpu.make_async_copy(blocks_ref, out_ref.at[pl.ds(0, blocks_dev)], sem).wait()


def pack(me, dest, blocks, owners):
    blocks_dev = blocks.shape[0]
    return pl.pallas_call(
        functools.partial(pack_kernel, owners, blocks_dev),
        out_shape=jax.ShapeDtypeStruct((owners * CAP,) + blocks.shape[1:], blocks.dtype),
        in_specs=[
            pl.BlockSpec(memory_space=pltpu.SMEM),
            pl.BlockSpec(memory_space=pltpu.SMEM),
            pl.BlockSpec(memory_space=pltpu.VMEM),
        ],
        out_specs=pl.BlockSpec(memory_space=pl.ANY),
        scratch_shapes=[pltpu.SMEM((owners,), jnp.int32), pltpu.SemaphoreType.DMA],
        name="pack",
    )(me, dest, blocks)


def plan_kernel(owners, blocks_dev, ao_blocks, me_ref, dest_ref, row_ref, col_ref, table_ref):
    me = me_ref[0]
    slots = owners * CAP
    cells = ao_blocks * ao_blocks

    def clear(c, _):
        table_ref[c] = slots
        return 0

    lax.fori_loop(0, cells, clear, 0)

    def source(s, total):
        def block(k, carry):
            rank, total = carry
            index = s * blocks_dev + k
            mine = dest_ref[index] == me

            @pl.when(mine)
            def _():
                slot = s * CAP + rank
                cell = row_ref[index] * ao_blocks + col_ref[index]
                table_ref[cells + slot] = table_ref[cell]
                table_ref[cell] = slot
                table_ref[cells + slots + 1 + total] = slot

            step = mine.astype(jnp.int32)
            return rank + step, total + step

        return lax.fori_loop(0, blocks_dev, block, (jnp.int32(0), total))[1]

    table_ref[cells + slots] = lax.fori_loop(0, owners, source, jnp.int32(0))


def plan(me, dest, row, col, owners, blocks_dev, ao_blocks):
    smem = pl.BlockSpec(memory_space=pltpu.SMEM)
    slots = owners * CAP
    return pl.pallas_call(
        functools.partial(plan_kernel, owners, blocks_dev, ao_blocks),
        out_shape=jax.ShapeDtypeStruct((ao_blocks * ao_blocks + 2 * slots + 1,), jnp.int32),
        in_specs=[smem] * 4,
        out_specs=smem,
        name="plan",
    )(me, dest, row, col)


def slab_kernel(
    slots, ao_blocks, table_ref, occ_ref, virt_ref, shuffle_ref, recv_ref, out_ref,
    held, dense, work, total, sem,
):
    width = ao_blocks * BA
    cells = ao_blocks * ao_blocks
    per_tile = LANES // BA
    tiles = width // LANES
    count = table_ref[cells + slots]

    def fetch(i, _):
        slot = table_ref[cells + slots + 1 + i]
        pltpu.make_async_copy(recv_ref.at[slot], held.at[slot], sem).start()
        return 0

    lax.fori_loop(0, count, fetch, 0)
    held[slots] = jnp.zeros(held.shape[1:], held.dtype)

    def arrive(i, _):
        pltpu.make_async_copy(recv_ref.at[0], held.at[0], sem).wait()
        return 0

    lax.fori_loop(0, count, arrive, 0)

    def merge(c, _):
        first = table_ref[c]

        @pl.when(first < slots)
        def _():
            second = table_ref[cells + first]

            @pl.when(second < slots)
            def _():
                total[...] = held[first].astype(jnp.float32)

                def add(slot):
                    total[...] += held[slot].astype(jnp.float32)
                    return table_ref[cells + slot]

                lax.while_loop(lambda slot: slot < slots, add, second)
                held[first] = total[...].astype(held.dtype)

        return 0

    lax.fori_loop(0, cells, merge, 0)

    shuffle = shuffle_ref[...]

    def place(step, _):
        r = step // tiles
        tile = step % tiles
        lanes = pl.ds(pl.multiple_of(tile * LANES, LANES), LANES)
        sources = [table_ref[r * ao_blocks + tile * per_tile + j] for j in range(per_tile)]
        x = jnp.concatenate(
            [
                jnp.concatenate([held[s, :, hi * LANES : (hi + 1) * LANES] for s in sources], axis=1)
                for hi in range(BA // per_tile)
            ],
            axis=0,
        )
        y = jnp.dot(x, shuffle, preferred_element_type=jnp.float32)
        for hi in range(BA // per_tile):
            for j in range(per_tile):
                mu = r * BA + hi * per_tile + j
                part = y[hi * BR : (hi + 1) * BR, j * LANES : (j + 1) * LANES]
                work[tile, pl.ds(mu * PITCH, BR), :] = part
                dense[mu, :, lanes] = part.astype(jnp.bfloat16)
        return 0

    lax.fori_loop(0, ao_blocks * tiles, place, 0)

    occ_t = occ_ref[...]
    virt = virt_ref[...]

    def transform(i, _):
        for j in range(8):
            rows = pl.ds(i * 8 + j, width, stride=PITCH)
            part = jnp.concatenate([work[t, rows, :] for t in range(tiles)], axis=1).astype(jnp.bfloat16)
            half = jnp.dot(occ_t, part, preferred_element_type=jnp.float32).astype(jnp.bfloat16)
            both = jnp.dot(half, virt, preferred_element_type=jnp.float32)
            for t in range(tiles):
                work[t, rows, :] = both[:, t * LANES : (t + 1) * LANES]
        return 0

    lax.fori_loop(0, BR // 8, transform, 0)

    def contract(i, acc):
        left, right = [], []
        for j in range(16):
            mu = i * 16 + j
            left += [work[t, pl.ds(mu * PITCH, BR), :] for t in range(tiles)]
            right.append(dense[mu])
        return acc + lax.dot_general(
            jnp.concatenate(left, axis=1).astype(jnp.bfloat16),
            jnp.concatenate(right, axis=1),
            (((1,), (1,)), ((), ())),
            preferred_element_type=jnp.float32,
        )

    out_ref[...] = lax.fori_loop(0, width // 16, contract, jnp.zeros((BR, BR), jnp.float32))


def slab(table, occ_t, virt, recv, ao_blocks):
    slots = recv.shape[0]
    width = ao_blocks * BA
    per_tile = LANES // BA
    smem = pl.BlockSpec(memory_space=pltpu.SMEM)
    vmem = pl.BlockSpec(memory_space=pltpu.VMEM)
    eye = jnp.eye(per_tile, dtype=jnp.bfloat16)
    shuffle = jnp.einsum("ac,bd,vw->abvdcw", eye, eye, jnp.eye(BA, dtype=jnp.bfloat16))
    shuffle = shuffle.reshape(per_tile * LANES, per_tile * LANES)
    return pl.pallas_call(
        functools.partial(slab_kernel, slots, ao_blocks),
        out_shape=jax.ShapeDtypeStruct((BR, BR), jnp.float32),
        in_specs=[smem, vmem, vmem, vmem, pl.BlockSpec(memory_space=pl.ANY)],
        out_specs=vmem,
        scratch_shapes=[
            pltpu.VMEM((slots + 1, BR, BA * BA), jnp.bfloat16),
            pltpu.VMEM((width, BR, width), jnp.bfloat16),
            pltpu.VMEM((width // LANES, width * PITCH, LANES), jnp.float32),
            pltpu.VMEM((BR, BA * BA), jnp.float32),
            pltpu.SemaphoreType.DMA,
        ],
        compiler_params=pltpu.CompilerParams(vmem_limit_bytes=48 * 1024 * 1024),
        name="slab",
    )(table, occ_t, virt, shuffle, recv)


def body(
    three_center, block_dest, block_row, block_col, occ_density, virt_density, occ_mask, virt_mask
):
    owners = lax.axis_size(("ri", "pair"))
    blocks_dev = three_center.shape[0]
    ao_blocks = occ_mask.shape[1]
    width = occ_density.shape[1]
    me = lax.axis_index(("ri", "pair")).astype(jnp.int32).reshape(1)
    dest = block_dest.reshape(-1)
    outgoing = pack(me, dest, three_center, owners)
    incoming = lax.all_to_all(outgoing, ("ri", "pair"), split_axis=0, concat_axis=0, tiled=True)
    local = jnp.concatenate(
        [
            occ_density * expand(occ_mask, BA).astype(jnp.bfloat16),
            virt_density * expand(virt_mask, BA).astype(jnp.bfloat16),
        ],
        axis=1,
    )
    whole = lax.all_gather(local, "orb", axis=0, tiled=True)
    table = plan(me, dest, block_row, block_col, owners, blocks_dev, ao_blocks)
    return slab(table, whole[:, :width].T, whole[:, width:], incoming, ao_blocks)


def solution(mesh):
    placed = (
        P(("orb", "ri", "pair"), None, None),
        P("orb", None),
        P("orb"),
        P("orb"),
        P("orb", None),
        P("orb", None),
        P("orb", None),
        P("orb", None),
    )
    return jax.shard_map(
        body, mesh=mesh, in_specs=placed, out_specs=P(("orb", "ri", "pair"), None), check_vma=False
    )
```

```python
import functools

import jax
import jax.numpy as jnp
from jax import lax
from jax.experimental import pallas as pl
from jax.experimental.pallas import tpu as pltpu
from jax.sharding import PartitionSpec as P

BR = 64
BA = 32
CAP = 2
LANES = 128
PITCH = BR + 1
OWNER_BITS = 5
RELAY_SPAN_BITS = 6
RELAY_SPAN = 1 << RELAY_SPAN_BITS
RELAY_MASKS = (4, 1, 3, 8, 24)
RELAY_CAPS = (12, 2, 2, 2, 2)


def expand(mask_blocks, block_width):
    return jnp.repeat(jnp.repeat(mask_blocks, block_width, axis=0), block_width, axis=1)


def relay_offsets():
    offsets, total = [], 0
    for cap in RELAY_CAPS:
        offsets.append(total)
        total += cap
    return offsets, total


def bit_of(word, index):
    return lax.shift_right_logical(word, index) & 1


def pack_kernel(
    owners, blocks_dev, me_ref, dest_ref, blocks_ref, out_ref, late_ref, route_ref,
    named_ref, direct_ref, second_ref, used_ref, place_ref, rank_ref, sem,
):
    me = me_ref[0]
    offsets, relays = relay_offsets()

    def start(s, total):
        named = jnp.int32(0)
        for k in range(blocks_dev):
            owner = dest_ref[s * blocks_dev + k]
            second_ref[total] = s * owners + owner
            total = total + bit_of(named, owner)
            named = named | lax.shift_left(jnp.int32(1), owner)
        named_ref[s] = named
        direct_ref[s] = named
        route_ref[s] = s
        route_ref[owners + s] = owners + relays + s
        place_ref[s] = s
        rank_ref[s] = 0
        for m in range(len(RELAY_MASKS)):
            used_ref[m * owners + s] = 0
        return total

    seconds = lax.fori_loop(0, owners, start, jnp.int32(0))
    head = 2 * owners
    route_ref[head + 1] = 0

    def record(s, via, owner, rank, mask_index, place):
        @pl.when(owner == me)
        def _():
            route_ref[rank * owners + s] = owners + place

        @pl.when(via == me)
        def _():
            count = route_ref[head + 1]
            route_ref[head + 2 + count] = s * RELAY_SPAN + place
            route_ref[head + 1] = count + 1

        @pl.when(s == me)
        def _():
            place_ref[rank * owners + owner] = via

    def room(mask_index, owner):
        return used_ref[mask_index * owners + owner] < RELAY_CAPS[mask_index]

    def route(e, failed):
        pair = second_ref[e]
        s, owner = lax.shift_right_logical(pair, OWNER_BITS), pair & (owners - 1)
        named = named_ref[s]
        near = owner ^ RELAY_MASKS[0]
        core_room = room(0, owner)
        choices = [(bit_of(named, near) == 0) & core_room]
        for m in range(1, len(RELAY_MASKS)):
            choices.append((bit_of(named, owner ^ RELAY_MASKS[m]) == 0) & room(m, owner))
        swap = core_room & (bit_of(direct_ref[s], near) == 1)
        for m in range(1, len(RELAY_MASKS)):
            choices.append(swap & (bit_of(named, near ^ RELAY_MASKS[m]) == 0) & room(m, near))
        choice = jnp.int32(len(choices))
        for c in reversed(range(len(choices))):
            choice = jnp.where(choices[c], jnp.int32(c), choice)
        for c in range(len(choices)):
            m = c if c < len(RELAY_MASKS) else c - len(RELAY_MASKS) + 1

            @pl.when(choice == c)
            def _():
                target = owner if c < len(RELAY_MASKS) else near
                via = target ^ RELAY_MASKS[m]
                count = used_ref[m * owners + target]
                used_ref[m * owners + target] = count + 1
                named_ref[s] = named | lax.shift_left(jnp.int32(1), via)
                record(s, via, target, 1 if c < len(RELAY_MASKS) else 0, m, offsets[m] + count)
                if c >= len(RELAY_MASKS):
                    direct_ref[s] = direct_ref[s] ^ lax.shift_left(jnp.int32(1), near)
                    count = used_ref[owner]
                    used_ref[owner] = count + 1
                    record(s, near, owner, 1, 0, offsets[0] + count)

        return failed | (choice == len(choices)).astype(jnp.int32)

    failed = lax.fori_loop(0, seconds, route, jnp.int32(0))
    route_ref[head] = failed

    @pl.when(failed == 1)
    def _():
        def undo(s, _):
            route_ref[s] = s
            route_ref[owners + s] = owners + relays + s
            place_ref[s] = s
            return 0

        lax.fori_loop(0, owners, undo, 0)
        route_ref[head + 1] = 0

    def send(k, _):
        owner = dest_ref[me * blocks_dev + k]
        rank = rank_ref[owner]
        rank_ref[owner] = rank + 1
        late = (rank == 1) & (failed == 1)

        @pl.when(late)
        def _():
            pltpu.make_async_copy(blocks_ref.at[k], late_ref.at[owner], sem).start()

        @pl.when(jnp.logical_not(late))
        def _():
            slot = place_ref[rank * owners + owner]
            pltpu.make_async_copy(blocks_ref.at[k], out_ref.at[slot], sem).start()

        return 0

    lax.fori_loop(0, blocks_dev, send, 0)
    pltpu.make_async_copy(blocks_ref, out_ref.at[pl.ds(0, blocks_dev)], sem).wait()


def pack(me, dest, blocks, owners):
    blocks_dev = blocks.shape[0]
    smem = pl.BlockSpec(memory_space=pltpu.SMEM)
    hbm = pl.BlockSpec(memory_space=pl.ANY)
    slots = jax.ShapeDtypeStruct((owners,) + blocks.shape[1:], blocks.dtype)
    relays = relay_offsets()[1]
    return pl.pallas_call(
        functools.partial(pack_kernel, owners, blocks_dev),
        out_shape=(slots, slots, jax.ShapeDtypeStruct((2 * owners + 2 + relays,), jnp.int32)),
        in_specs=[smem, smem, pl.BlockSpec(memory_space=pltpu.VMEM)],
        out_specs=(hbm, hbm, smem),
        scratch_shapes=[
            pltpu.SMEM((owners,), jnp.int32),
            pltpu.SMEM((owners,), jnp.int32),
            pltpu.SMEM((owners * blocks_dev,), jnp.int32),
            pltpu.SMEM((len(RELAY_MASKS) * owners,), jnp.int32),
            pltpu.SMEM((2 * owners,), jnp.int32),
            pltpu.SMEM((owners,), jnp.int32),
            pltpu.SemaphoreType.DMA,
        ],
        name="pack",
    )(me, dest, blocks)


def forward_kernel(owners, route_ref, recv_ref, *refs):
    relay_refs, stage_ref, sem = refs[: len(RELAY_MASKS)], refs[-2], refs[-1]
    offsets, relays = relay_offsets()
    head = 2 * owners
    count = route_ref[head + 1]

    def take(i, _):
        slot = lax.shift_right_logical(route_ref[head + 2 + i], RELAY_SPAN_BITS)
        pltpu.make_async_copy(recv_ref.at[slot], stage_ref.at[i], sem).start()
        return 0

    def give(i, _):
        place = route_ref[head + 2 + i] & (RELAY_SPAN - 1)
        for ref, offset, cap in zip(relay_refs, offsets, RELAY_CAPS):
            @pl.when((place >= offset) & (place < offset + cap))
            def _():
                pltpu.make_async_copy(stage_ref.at[i], ref.at[place - offset], sem).start()

        return 0

    def wait(i, _):
        pltpu.make_async_copy(recv_ref.at[0], stage_ref.at[0], sem).wait()
        return 0

    lax.fori_loop(0, count, take, 0)
    lax.fori_loop(0, count, wait, 0)
    lax.fori_loop(0, count, give, 0)
    lax.fori_loop(0, count, wait, 0)


def forward(route, recv):
    owners = recv.shape[0]
    hbm = pl.BlockSpec(memory_space=pl.ANY)
    block = recv.shape[1:]
    return pl.pallas_call(
        functools.partial(forward_kernel, owners),
        out_shape=tuple(jax.ShapeDtypeStruct((cap,) + block, recv.dtype) for cap in RELAY_CAPS),
        in_specs=[pl.BlockSpec(memory_space=pltpu.SMEM), hbm],
        out_specs=(hbm,) * len(RELAY_CAPS),
        scratch_shapes=[pltpu.VMEM((relay_offsets()[1],) + block, recv.dtype), pltpu.SemaphoreType.DMA],
        name="forward",
    )(route, recv)


def plan_kernel(owners, blocks_dev, ao_blocks, me_ref, dest_ref, row_ref, col_ref, route_ref, table_ref):
    me = me_ref[0]
    most = owners * CAP
    cells = ao_blocks * ao_blocks

    def clear(c, _):
        table_ref[c] = most
        return 0

    lax.fori_loop(0, cells, clear, 0)

    def source(s, total):
        def block(k, carry):
            rank, total = carry
            index = s * blocks_dev + k
            mine = dest_ref[index] == me

            @pl.when(mine)
            def _():
                cell = row_ref[index] * ao_blocks + col_ref[index]
                table_ref[cells + total] = table_ref[cell]
                table_ref[cell] = total
                table_ref[cells + most + total] = route_ref[rank * owners + s]

            step = mine.astype(jnp.int32)
            return rank + step, total + step

        return lax.fori_loop(0, blocks_dev, block, (jnp.int32(0), total))[1]

    table_ref[cells + 2 * most] = lax.fori_loop(0, owners, source, jnp.int32(0))


def plan(me, dest, row, col, route, owners, blocks_dev, ao_blocks):
    smem = pl.BlockSpec(memory_space=pltpu.SMEM)
    most = owners * CAP
    return pl.pallas_call(
        functools.partial(plan_kernel, owners, blocks_dev, ao_blocks),
        out_shape=jax.ShapeDtypeStruct((ao_blocks * ao_blocks + 2 * most + 1,), jnp.int32),
        in_specs=[smem] * 5,
        out_specs=smem,
        name="plan",
    )(me, dest, row, col, route)


def slab_kernel(
    most, ao_blocks, table_ref, occ_ref, virt_ref, shuffle_ref, *refs
):
    recv_refs = refs[:-6]
    out_ref, held, dense, work, total, sem = refs[-6:]
    width = ao_blocks * BA
    cells = ao_blocks * ao_blocks
    per_tile = LANES // BA
    tiles = width // LANES
    count = table_ref[cells + 2 * most]

    def fetch(i, _):
        place = table_ref[cells + most + i]
        offset = 0
        for ref in recv_refs:
            @pl.when((place >= offset) & (place < offset + ref.shape[0]))
            def _():
                pltpu.make_async_copy(ref.at[place - offset], held.at[i], sem).start()

            offset += ref.shape[0]
        return 0

    lax.fori_loop(0, count, fetch, 0)
    held[most] = jnp.zeros(held.shape[1:], held.dtype)

    def arrive(i, _):
        pltpu.make_async_copy(recv_refs[0].at[0], held.at[0], sem).wait()
        return 0

    lax.fori_loop(0, count, arrive, 0)

    def merge(c, _):
        first = table_ref[c]

        @pl.when(first < most)
        def _():
            second = table_ref[cells + first]

            @pl.when(second < most)
            def _():
                total[...] = held[first].astype(jnp.float32)

                def add(slot):
                    total[...] += held[slot].astype(jnp.float32)
                    return table_ref[cells + slot]

                lax.while_loop(lambda slot: slot < most, add, second)
                held[first] = total[...].astype(held.dtype)

        return 0

    lax.fori_loop(0, cells, merge, 0)

    shuffle = shuffle_ref[...]

    def place(step, _):
        r = step // tiles
        tile = step % tiles
        lanes = pl.ds(pl.multiple_of(tile * LANES, LANES), LANES)
        sources = [table_ref[r * ao_blocks + tile * per_tile + j] for j in range(per_tile)]
        x = jnp.concatenate(
            [
                jnp.concatenate([held[s, :, hi * LANES : (hi + 1) * LANES] for s in sources], axis=1)
                for hi in range(BA // per_tile)
            ],
            axis=0,
        )
        y = jnp.dot(x, shuffle, preferred_element_type=jnp.float32)
        for hi in range(BA // per_tile):
            for j in range(per_tile):
                mu = r * BA + hi * per_tile + j
                part = y[hi * BR : (hi + 1) * BR, j * LANES : (j + 1) * LANES]
                work[tile, pl.ds(mu * PITCH, BR), :] = part
                dense[mu, :, lanes] = part.astype(jnp.bfloat16)
        return 0

    lax.fori_loop(0, ao_blocks * tiles, place, 0)

    occ_t = occ_ref[...]
    virt = virt_ref[...]

    def transform(i, _):
        for j in range(8):
            rows = pl.ds(i * 8 + j, width, stride=PITCH)
            part = jnp.concatenate([work[t, rows, :] for t in range(tiles)], axis=1).astype(jnp.bfloat16)
            half = jnp.dot(occ_t, part, preferred_element_type=jnp.float32).astype(jnp.bfloat16)
            both = jnp.dot(half, virt, preferred_element_type=jnp.float32)
            for t in range(tiles):
                work[t, rows, :] = both[:, t * LANES : (t + 1) * LANES]
        return 0

    lax.fori_loop(0, BR // 8, transform, 0)

    def contract(i, acc):
        left, right = [], []
        for j in range(16):
            mu = i * 16 + j
            left += [work[t, pl.ds(mu * PITCH, BR), :] for t in range(tiles)]
            right.append(dense[mu])
        return acc + lax.dot_general(
            jnp.concatenate(left, axis=1).astype(jnp.bfloat16),
            jnp.concatenate(right, axis=1),
            (((1,), (1,)), ((), ())),
            preferred_element_type=jnp.float32,
        )

    out_ref[...] = lax.fori_loop(0, width // 16, contract, jnp.zeros((BR, BR), jnp.float32))


def slab(table, occ_t, virt, received, most, ao_blocks):
    width = ao_blocks * BA
    per_tile = LANES // BA
    smem = pl.BlockSpec(memory_space=pltpu.SMEM)
    vmem = pl.BlockSpec(memory_space=pltpu.VMEM)
    eye = jnp.eye(per_tile, dtype=jnp.bfloat16)
    shuffle = jnp.einsum("ac,bd,vw->abvdcw", eye, eye, jnp.eye(BA, dtype=jnp.bfloat16))
    shuffle = shuffle.reshape(per_tile * LANES, per_tile * LANES)
    return pl.pallas_call(
        functools.partial(slab_kernel, most, ao_blocks),
        out_shape=jax.ShapeDtypeStruct((BR, BR), jnp.float32),
        in_specs=[smem, vmem, vmem, vmem] + [pl.BlockSpec(memory_space=pl.ANY)] * len(received),
        out_specs=vmem,
        scratch_shapes=[
            pltpu.VMEM((most + 1, BR, BA * BA), jnp.bfloat16),
            pltpu.VMEM((width, BR, width), jnp.bfloat16),
            pltpu.VMEM((width // LANES, width * PITCH, LANES), jnp.float32),
            pltpu.VMEM((BR, BA * BA), jnp.float32),
            pltpu.SemaphoreType.DMA,
        ],
        compiler_params=pltpu.CompilerParams(vmem_limit_bytes=48 * 1024 * 1024),
        name="slab",
    )(table, occ_t, virt, shuffle, *received)


def body(
    three_center, block_dest, block_row, block_col, occ_density, virt_density, occ_mask, virt_mask
):
    owners = lax.axis_size(("ri", "pair"))
    blocks_dev = three_center.shape[0]
    ao_blocks = occ_mask.shape[1]
    width = occ_density.shape[1]
    me = lax.axis_index(("ri", "pair")).astype(jnp.int32).reshape(1)
    dest = block_dest.reshape(-1)
    outgoing, late, route = pack(me, dest, three_center, owners)
    group = ("ri", "pair")

    def exchange(slots):
        return lax.all_to_all(slots, group, split_axis=0, concat_axis=0, tiled=True)

    incoming = exchange(outgoing)
    local = jnp.concatenate(
        [
            occ_density * expand(occ_mask, BA).astype(jnp.bfloat16),
            virt_density * expand(virt_mask, BA).astype(jnp.bfloat16),
        ],
        axis=1,
    )
    need_late = jnp.broadcast_to(route[2 * owners].astype(jnp.bfloat16), (8, 2 * width))
    height = local.shape[0]
    gathered = lax.all_gather(jnp.concatenate([local, need_late], axis=0), "orb", axis=0, tiled=True)
    gathered = gathered.reshape(-1, height + 8, 2 * width)
    whole = gathered[:, :height].reshape(width, 2 * width)
    any_late = jnp.max(gathered[:, height, 0]) > 0
    table = plan(me, dest, block_row, block_col, route, owners, blocks_dev, ao_blocks)
    route, table, occ_t, virt, any_late = lax.optimization_barrier(
        (route, table, whole[:, :width].T, whole[:, width:], any_late)
    )
    incoming, late = lax.optimization_barrier((incoming, late))
    late = lax.cond(any_late, exchange, lambda slots: slots, late)
    relayed = [
        lax.ppermute(part, group, [(i, i ^ mask) for i in range(owners)])
        for part, mask in zip(forward(route, incoming), RELAY_MASKS)
    ]
    return slab(table, occ_t, virt, [incoming, *relayed, late], owners * CAP, ao_blocks)


def solution(mesh):
    placed = (
        P(("orb", "ri", "pair"), None, None),
        P("orb", None),
        P("orb"),
        P("orb"),
        P("orb", None),
        P("orb", None),
        P("orb", None),
        P("orb", None),
    )
    return jax.shard_map(
        body, mesh=mesh, in_specs=placed, out_specs=P(("orb", "ri", "pair"), None), check_vma=False
    )
```

```python
import functools

import jax
import jax.numpy as jnp
from jax import lax
from jax.experimental import pallas as pl
from jax.experimental.pallas import tpu as pltpu
from jax.sharding import PartitionSpec as P

BR = 64
BA = 32
CAP = 2
LANES = 128
PITCH = BR + 1
OWNER_BITS = 5
RELAY_SPAN_BITS = 6
RELAY_SPAN = 1 << RELAY_SPAN_BITS
RELAY_MASKS = (4, 1, 3, 8, 24)
RELAY_CAPS = (12, 2, 2, 2, 2)
NEAR_SHIFT = 4
NEAR_LOW = 0x0F0F0F0F
PLACE_BITS = 7


def expand(mask_blocks, block_width):
    return jnp.repeat(jnp.repeat(mask_blocks, block_width, axis=0), block_width, axis=1)


def relay_offsets():
    offsets, total = [], 0
    for cap in RELAY_CAPS:
        offsets.append(total)
        total += cap
    return offsets, total


def bit_of(word, index):
    return lax.shift_right_logical(word, index) & 1


def pack_kernel(
    owners, blocks_dev, me_ref, dest_ref, blocks_ref, out_ref, late_ref, route_ref,
    named_ref, direct_ref, second_ref, used_ref, place_ref, rank_ref, kept_ref, sem,
):
    me = me_ref[0]
    offsets, relays = relay_offsets()

    def tally(s):
        bits = [lax.shift_left(jnp.int32(1), dest_ref[s * blocks_dev + k]) for k in range(blocks_dev)]
        named = functools.reduce(lax.bitwise_or, bits)
        return named, functools.reduce(lax.add, bits) - named

    def clear(o, _):
        rank_ref[o] = 0
        return 0

    lax.fori_loop(0, owners, clear, 0)
    twice = tally(me)[1]
    low = jnp.int32(NEAR_LOW)
    near_twice = lax.shift_left(twice & low, NEAR_SHIFT) | (lax.shift_right_logical(twice, NEAR_SHIFT) & low)

    def send_early(k, _):
        owner = dest_ref[me * blocks_dev + k]
        rank = rank_ref[owner]
        rank_ref[owner] = rank + 1
        early = (rank == 0) & (bit_of(near_twice, owner) == 0)
        kept_ref[k] = jnp.where(early, -1, rank)

        @pl.when(early)
        def _():
            pltpu.make_async_copy(blocks_ref.at[k], out_ref.at[owner], sem).start()

        return 0

    lax.fori_loop(0, blocks_dev, send_early, 0)

    def list_seconds(s, total):
        seen = jnp.int32(0)
        for k in range(blocks_dev):
            owner = dest_ref[s * blocks_dev + k]
            second_ref[total] = s * owners + owner
            total = total + bit_of(seen, owner)
            seen = seen | lax.shift_left(jnp.int32(1), owner)
        return total

    def start(s, total):
        named, doubled = tally(s)
        total = lax.cond(doubled != 0, lambda: list_seconds(s, total), lambda: total)
        named_ref[s] = named
        direct_ref[s] = named
        route_ref[s] = s
        route_ref[owners + s] = owners + relays + s
        place_ref[s] = s
        for m in range(len(RELAY_MASKS)):
            used_ref[m * owners + s] = 0
        return total

    seconds = lax.fori_loop(0, owners, start, jnp.int32(0))
    head = 2 * owners
    route_ref[head + 1] = 0

    def record(s, via, owner, rank, mask_index, place):
        @pl.when(owner == me)
        def _():
            route_ref[rank * owners + s] = owners + place

        @pl.when(via == me)
        def _():
            count = route_ref[head + 1]
            route_ref[head + 2 + count] = s * RELAY_SPAN + place
            route_ref[head + 1] = count + 1

        @pl.when(s == me)
        def _():
            place_ref[rank * owners + owner] = via

    def room(mask_index, owner):
        return used_ref[mask_index * owners + owner] < RELAY_CAPS[mask_index]

    def route(e, failed):
        pair = second_ref[e]
        s, owner = lax.shift_right_logical(pair, OWNER_BITS), pair & (owners - 1)
        named = named_ref[s]
        near = owner ^ RELAY_MASKS[0]
        core_room = room(0, owner)
        choices = [(bit_of(named, near) == 0) & core_room]
        for m in range(1, len(RELAY_MASKS)):
            choices.append((bit_of(named, owner ^ RELAY_MASKS[m]) == 0) & room(m, owner))
        swap = core_room & (bit_of(direct_ref[s], near) == 1)
        for m in range(1, len(RELAY_MASKS)):
            choices.append(swap & (bit_of(named, near ^ RELAY_MASKS[m]) == 0) & room(m, near))
        choice = jnp.int32(len(choices))
        for c in reversed(range(len(choices))):
            choice = jnp.where(choices[c], jnp.int32(c), choice)
        for c in range(len(choices)):
            m = c if c < len(RELAY_MASKS) else c - len(RELAY_MASKS) + 1

            @pl.when(choice == c)
            def _():
                target = owner if c < len(RELAY_MASKS) else near
                via = target ^ RELAY_MASKS[m]
                count = used_ref[m * owners + target]
                used_ref[m * owners + target] = count + 1
                named_ref[s] = named | lax.shift_left(jnp.int32(1), via)
                record(s, via, target, 1 if c < len(RELAY_MASKS) else 0, m, offsets[m] + count)
                if c >= len(RELAY_MASKS):
                    direct_ref[s] = direct_ref[s] ^ lax.shift_left(jnp.int32(1), near)
                    count = used_ref[owner]
                    used_ref[owner] = count + 1
                    record(s, near, owner, 1, 0, offsets[0] + count)

        return failed | (choice == len(choices)).astype(jnp.int32)

    failed = lax.fori_loop(0, seconds, route, jnp.int32(0))
    route_ref[head] = failed

    @pl.when(failed == 1)
    def _():
        def undo(s, _):
            route_ref[s] = s
            route_ref[owners + s] = owners + relays + s
            place_ref[s] = s
            return 0

        lax.fori_loop(0, owners, undo, 0)
        route_ref[head + 1] = 0

    def send(k, _):
        rank = kept_ref[k]

        @pl.when(rank >= 0)
        def _():
            owner = dest_ref[me * blocks_dev + k]
            late = (rank == 1) & (failed == 1)

            @pl.when(late)
            def _():
                pltpu.make_async_copy(blocks_ref.at[k], late_ref.at[owner], sem).start()

            @pl.when(jnp.logical_not(late))
            def _():
                slot = place_ref[rank * owners + owner]
                pltpu.make_async_copy(blocks_ref.at[k], out_ref.at[slot], sem).start()

        return 0

    lax.fori_loop(0, blocks_dev, send, 0)
    pltpu.make_async_copy(blocks_ref, out_ref.at[pl.ds(0, blocks_dev)], sem).wait()


def pack(me, dest, blocks, owners):
    blocks_dev = blocks.shape[0]
    smem = pl.BlockSpec(memory_space=pltpu.SMEM)
    hbm = pl.BlockSpec(memory_space=pl.ANY)
    slots = jax.ShapeDtypeStruct((owners,) + blocks.shape[1:], blocks.dtype)
    relays = relay_offsets()[1]
    return pl.pallas_call(
        functools.partial(pack_kernel, owners, blocks_dev),
        out_shape=(slots, slots, jax.ShapeDtypeStruct((2 * owners + 2 + relays,), jnp.int32)),
        in_specs=[smem, smem, pl.BlockSpec(memory_space=pltpu.VMEM)],
        out_specs=(hbm, hbm, smem),
        scratch_shapes=[
            pltpu.SMEM((owners,), jnp.int32),
            pltpu.SMEM((owners,), jnp.int32),
            pltpu.SMEM((owners * blocks_dev,), jnp.int32),
            pltpu.SMEM((len(RELAY_MASKS) * owners,), jnp.int32),
            pltpu.SMEM((2 * owners,), jnp.int32),
            pltpu.SMEM((owners,), jnp.int32),
            pltpu.SMEM((blocks_dev,), jnp.int32),
            pltpu.SemaphoreType.DMA,
        ],
        name="pack",
    )(me, dest, blocks)


def forward_kernel(owners, route_ref, recv_ref, *refs):
    relay_refs, stage_ref, sem = refs[: len(RELAY_MASKS)], refs[-2], refs[-1]
    offsets, relays = relay_offsets()
    head = 2 * owners
    count = route_ref[head + 1]

    def take(i, _):
        slot = lax.shift_right_logical(route_ref[head + 2 + i], RELAY_SPAN_BITS)
        pltpu.make_async_copy(recv_ref.at[slot], stage_ref.at[i], sem).start()
        return 0

    def give(i, _):
        place = route_ref[head + 2 + i] & (RELAY_SPAN - 1)
        for ref, offset, cap in zip(relay_refs, offsets, RELAY_CAPS):
            @pl.when((place >= offset) & (place < offset + cap))
            def _():
                pltpu.make_async_copy(stage_ref.at[i], ref.at[place - offset], sem).start()

        return 0

    def wait(i, _):
        pltpu.make_async_copy(recv_ref.at[0], stage_ref.at[0], sem).wait()
        return 0

    lax.fori_loop(0, count, take, 0)
    lax.fori_loop(0, count, wait, 0)
    lax.fori_loop(0, count, give, 0)
    lax.fori_loop(0, count, wait, 0)


def forward(route, recv):
    owners = recv.shape[0]
    hbm = pl.BlockSpec(memory_space=pl.ANY)
    block = recv.shape[1:]
    return pl.pallas_call(
        functools.partial(forward_kernel, owners),
        out_shape=tuple(jax.ShapeDtypeStruct((cap,) + block, recv.dtype) for cap in RELAY_CAPS),
        in_specs=[pl.BlockSpec(memory_space=pltpu.SMEM), hbm],
        out_specs=(hbm,) * len(RELAY_CAPS),
        scratch_shapes=[pltpu.VMEM((relay_offsets()[1],) + block, recv.dtype), pltpu.SemaphoreType.DMA],
        name="forward",
    )(route, recv)


def plan_kernel(owners, blocks_dev, ao_blocks, me_ref, dest_ref, row_ref, col_ref, route_ref, table_ref):
    me = me_ref[0]
    most = owners * CAP
    cells = ao_blocks * ao_blocks

    def clear(c, _):
        table_ref[c] = most
        return 0

    lax.fori_loop(0, cells, clear, 0)
    tail = cells + 2 * most + 1
    for r in range(ao_blocks):
        table_ref[tail + r] = 0

    def source(s, total):
        def block(k, carry):
            rank, total = carry
            index = s * blocks_dev + k
            mine = dest_ref[index] == me

            @pl.when(mine)
            def _():
                row = row_ref[index]
                cell = row * ao_blocks + col_ref[index]
                table_ref[cells + total] = table_ref[cell]
                table_ref[cell] = total
                place = route_ref[rank * owners + s]
                table_ref[cells + most + total] = place | lax.shift_left(row, PLACE_BITS)
                table_ref[tail + row] += 1

            step = mine.astype(jnp.int32)
            return rank + step, total + step

        return lax.fori_loop(0, blocks_dev, block, (jnp.int32(0), total))[1]

    table_ref[cells + 2 * most] = lax.fori_loop(0, owners, source, jnp.int32(0))


def plan(me, dest, row, col, route, owners, blocks_dev, ao_blocks):
    smem = pl.BlockSpec(memory_space=pltpu.SMEM)
    most = owners * CAP
    return pl.pallas_call(
        functools.partial(plan_kernel, owners, blocks_dev, ao_blocks),
        out_shape=jax.ShapeDtypeStruct((ao_blocks * ao_blocks + 2 * most + 1 + ao_blocks,), jnp.int32),
        in_specs=[smem] * 5,
        out_specs=smem,
        name="plan",
    )(me, dest, row, col, route)


def slab_kernel(
    most, ao_blocks, table_ref, occ_ref, virt_ref, shuffle_ref, *refs
):
    recv_refs = refs[:-6]
    out_ref, held, dense, work, total, sem = refs[-6:]
    width = ao_blocks * BA
    cells = ao_blocks * ao_blocks
    per_tile = LANES // BA
    tiles = width // LANES
    count = table_ref[cells + 2 * most]

    def fetch(i, _):
        entry = table_ref[cells + most + i]
        place = entry & ((1 << PLACE_BITS) - 1)
        row = lax.shift_right_logical(entry, PLACE_BITS)
        slots = recv_refs[0].shape[0]

        @pl.when(place < slots)
        def _():
            pltpu.make_async_copy(recv_refs[0].at[place], held.at[i], sem.at[row]).start()

        @pl.when(place >= slots)
        def _():
            offset = slots
            for ref in recv_refs[1:]:
                @pl.when((place >= offset) & (place < offset + ref.shape[0]))
                def _():
                    pltpu.make_async_copy(ref.at[place - offset], held.at[i], sem.at[row]).start()

                offset += ref.shape[0]

        return 0

    lax.fori_loop(0, count, fetch, 0)
    held[most] = jnp.zeros(held.shape[1:], held.dtype)

    def merge(c, _):
        first = table_ref[c]

        @pl.when(first < most)
        def _():
            second = table_ref[cells + first]

            @pl.when(second < most)
            def _():
                total[...] = held[first].astype(jnp.float32)

                def add(slot):
                    total[...] += held[slot].astype(jnp.float32)
                    return table_ref[cells + slot]

                lax.while_loop(lambda slot: slot < most, add, second)
                held[first] = total[...].astype(held.dtype)

        return 0

    shuffle = shuffle_ref[...]

    def place(r, _):
        def arrive(i, _):
            pltpu.make_async_copy(recv_refs[0].at[0], held.at[0], sem.at[r]).wait()
            return 0

        lax.fori_loop(0, table_ref[cells + 2 * most + 1 + r], arrive, 0)
        lax.fori_loop(r * ao_blocks, (r + 1) * ao_blocks, merge, 0)
        for tile in range(tiles):
            lanes = slice(tile * LANES, (tile + 1) * LANES)
            sources = [table_ref[r * ao_blocks + tile * per_tile + j] for j in range(per_tile)]
            x = jnp.concatenate(
                [
                    jnp.concatenate([held[s, :, hi * LANES : (hi + 1) * LANES] for s in sources], axis=1)
                    for hi in range(BA // per_tile)
                ],
                axis=0,
            )
            y = jnp.dot(x, shuffle, preferred_element_type=jnp.float32)
            for hi in range(BA // per_tile):
                for j in range(per_tile):
                    mu = r * BA + hi * per_tile + j
                    part = y[hi * BR : (hi + 1) * BR, j * LANES : (j + 1) * LANES]
                    work[tile, pl.ds(mu * PITCH, BR), :] = part
                    dense[mu, :, lanes] = part.astype(jnp.bfloat16)
        return 0

    lax.fori_loop(0, ao_blocks, place, 0)

    occ_t = occ_ref[...].astype(jnp.float32).T.astype(jnp.bfloat16)
    virt = virt_ref[...]

    def transform(i, _):
        for j in range(16):
            rows = pl.ds(i * 16 + j, width, stride=PITCH)
            part = jnp.concatenate([work[t, rows, :] for t in range(tiles)], axis=1).astype(jnp.bfloat16)
            half = jnp.dot(occ_t, part, preferred_element_type=jnp.float32).astype(jnp.bfloat16)
            both = jnp.dot(half, virt, preferred_element_type=jnp.float32)
            for t in range(tiles):
                work[t, rows, :] = both[:, t * LANES : (t + 1) * LANES]
        return 0

    lax.fori_loop(0, BR // 16, transform, 0)

    def contract(i, acc):
        left, right = [], []
        for j in range(32):
            mu = i * 32 + j
            left += [work[t, pl.ds(mu * PITCH, BR), :] for t in range(tiles)]
            right.append(dense[mu])
        return acc + lax.dot_general(
            jnp.concatenate(left, axis=1).astype(jnp.bfloat16),
            jnp.concatenate(right, axis=1),
            (((1,), (1,)), ((), ())),
            preferred_element_type=jnp.float32,
        )

    out_ref[...] = lax.fori_loop(0, width // 32, contract, jnp.zeros((BR, BR), jnp.float32))


def lane_shuffle():
    side = LANES // BA
    lane, to = (lax.broadcasted_iota(jnp.int32, (side * LANES, side * LANES), axis) for axis in (0, 1))
    target = ((lane >> 5) & (side - 1)) * LANES + (lane >> 7) * BA + (lane & (BA - 1))
    return (to == target).astype(jnp.bfloat16)


def slab(table, occ, virt, shuffle, received, most, ao_blocks):
    width = ao_blocks * BA
    smem = pl.BlockSpec(memory_space=pltpu.SMEM)
    vmem = pl.BlockSpec(memory_space=pltpu.VMEM)
    return pl.pallas_call(
        functools.partial(slab_kernel, most, ao_blocks),
        out_shape=jax.ShapeDtypeStruct((BR, BR), jnp.float32),
        in_specs=[smem, vmem, vmem, vmem] + [pl.BlockSpec(memory_space=pl.ANY)] * len(received),
        out_specs=vmem,
        scratch_shapes=[
            pltpu.VMEM((most + 1, BR, BA * BA), jnp.bfloat16),
            pltpu.VMEM((width, BR, width), jnp.bfloat16),
            pltpu.VMEM((width // LANES, width * PITCH, LANES), jnp.float32),
            pltpu.VMEM((BR, BA * BA), jnp.float32),
            pltpu.SemaphoreType.DMA((ao_blocks,)),
        ],
        compiler_params=pltpu.CompilerParams(vmem_limit_bytes=48 * 1024 * 1024),
        name="slab",
    )(table, occ, virt, shuffle, *received)


def body(
    three_center, block_dest, block_row, block_col, occ_density, virt_density, occ_mask, virt_mask
):
    owners = lax.axis_size(("ri", "pair"))
    blocks_dev = three_center.shape[0]
    ao_blocks = occ_mask.shape[1]
    width = occ_density.shape[1]
    me = lax.axis_index(("ri", "pair")).astype(jnp.int32).reshape(1)
    dest = block_dest.reshape(-1)
    outgoing, late, route = pack(me, dest, three_center, owners)
    group = ("ri", "pair")

    def exchange(slots):
        return lax.all_to_all(slots, group, split_axis=0, concat_axis=0, tiled=True)

    incoming = exchange(outgoing)
    local = jnp.concatenate(
        [
            occ_density * expand(occ_mask, BA).astype(jnp.bfloat16),
            virt_density * expand(virt_mask, BA).astype(jnp.bfloat16),
        ],
        axis=1,
    )
    need_late = jnp.broadcast_to(route[2 * owners].astype(jnp.bfloat16), (8, 2 * width))
    height = local.shape[0]
    gathered = lax.all_gather(jnp.concatenate([local, need_late], axis=0), "orb", axis=0, tiled=True)
    gathered = gathered.reshape(-1, height + 8, 2 * width)
    whole = gathered[:, :height].reshape(width, 2 * width)
    any_late = jnp.max(gathered[:, height, 0]) > 0
    table = plan(me, dest, block_row, block_col, route, owners, blocks_dev, ao_blocks)
    route, table, occ, virt, shuffle, any_late = lax.optimization_barrier(
        (route, table, whole[:, :width], whole[:, width:], lane_shuffle(), any_late)
    )
    incoming, late = lax.optimization_barrier((incoming, late))
    late = lax.cond(any_late, exchange, lambda slots: slots, late)
    relayed = [
        lax.ppermute(part, group, [(i, i ^ mask) for i in range(owners)])
        for part, mask in zip(forward(route, incoming), RELAY_MASKS)
    ]
    return slab(table, occ, virt, shuffle, [incoming, *relayed, late], owners * CAP, ao_blocks)


def solution(mesh):
    placed = (
        P(("orb", "ri", "pair"), None, None),
        P("orb", None),
        P("orb"),
        P("orb"),
        P("orb", None),
        P("orb", None),
        P("orb", None),
        P("orb", None),
    )
    return jax.shard_map(
        body, mesh=mesh, in_specs=placed, out_specs=P(("orb", "ri", "pair"), None), check_vma=False
    )
```

```python
import functools

import jax
import jax.numpy as jnp
from jax import lax
from jax.experimental import pallas as pl
from jax.experimental.pallas import tpu as pltpu
from jax.sharding import PartitionSpec as P

BR = 64
BA = 32
CAP = 2
LANES = 128
PITCH = BR + 1
OWNER_BITS = 5
RELAY_SPAN_BITS = 6
RELAY_SPAN = 1 << RELAY_SPAN_BITS
RELAY_MASKS = (4, 1, 3, 8, 24)
RELAY_CAPS = (12, 2, 2, 2, 2)
NEAR_SHIFT = 4
NEAR_LOW = 0x0F0F0F0F
PLACE_BITS = 7
GROUP_BITS = 2
SCOPED = 12 * 1024 * 1024


def expand(mask_blocks, block_width):
    return jnp.repeat(jnp.repeat(mask_blocks, block_width, axis=0), block_width, axis=1)


def relay_offsets():
    offsets, total = [], 0
    for cap in RELAY_CAPS:
        offsets.append(total)
        total += cap
    return offsets, total


def groups_of(ao_blocks):
    return ao_blocks * ao_blocks >> GROUP_BITS


def bit_of(word, index):
    return lax.shift_right_logical(word, index) & 1


def pack_kernel(
    owners, blocks_dev, me_ref, dest_ref, blocks_ref, out_ref, late_ref, route_ref,
    named_ref, direct_ref, second_ref, used_ref, place_ref, rank_ref, kept_ref, sem,
):
    me = me_ref[0]
    offsets, relays = relay_offsets()

    def tally(s):
        bits = [lax.shift_left(jnp.int32(1), dest_ref[s * blocks_dev + k]) for k in range(blocks_dev)]
        named = functools.reduce(lax.bitwise_or, bits)
        return named, functools.reduce(lax.add, bits) - named

    def clear(o, _):
        rank_ref[o] = 0
        return 0

    lax.fori_loop(0, owners, clear, 0)
    twice = tally(me)[1]
    low = jnp.int32(NEAR_LOW)
    near_twice = lax.shift_left(twice & low, NEAR_SHIFT) | (lax.shift_right_logical(twice, NEAR_SHIFT) & low)

    def send_early(k, _):
        owner = dest_ref[me * blocks_dev + k]
        rank = rank_ref[owner]
        rank_ref[owner] = rank + 1
        early = (rank == 0) & (bit_of(near_twice, owner) == 0)
        kept_ref[k] = jnp.where(early, -1, rank)

        @pl.when(early)
        def _():
            pltpu.make_async_copy(blocks_ref.at[k], out_ref.at[owner], sem).start()

        return 0

    lax.fori_loop(0, blocks_dev, send_early, 0)

    def list_seconds(s, total):
        seen = jnp.int32(0)
        for k in range(blocks_dev):
            owner = dest_ref[s * blocks_dev + k]
            second_ref[total] = s * owners + owner
            total = total + bit_of(seen, owner)
            seen = seen | lax.shift_left(jnp.int32(1), owner)
        return total

    def start(s, total):
        named, doubled = tally(s)
        total = lax.cond(doubled != 0, lambda: list_seconds(s, total), lambda: total)
        named_ref[s] = named
        direct_ref[s] = named
        route_ref[s] = s
        route_ref[owners + s] = owners + relays + s
        place_ref[s] = s
        for m in range(len(RELAY_MASKS)):
            used_ref[m * owners + s] = 0
        return total

    seconds = lax.fori_loop(0, owners, start, jnp.int32(0))
    head = 2 * owners
    route_ref[head + 1] = 0

    def record(s, via, owner, rank, mask_index, place):
        @pl.when(owner == me)
        def _():
            route_ref[rank * owners + s] = owners + place

        @pl.when(via == me)
        def _():
            count = route_ref[head + 1]
            route_ref[head + 2 + count] = s * RELAY_SPAN + place
            route_ref[head + 1] = count + 1

        @pl.when(s == me)
        def _():
            place_ref[rank * owners + owner] = via

    def room(mask_index, owner):
        return used_ref[mask_index * owners + owner] < RELAY_CAPS[mask_index]

    def route(e, failed):
        pair = second_ref[e]
        s, owner = lax.shift_right_logical(pair, OWNER_BITS), pair & (owners - 1)
        named = named_ref[s]
        near = owner ^ RELAY_MASKS[0]
        core_room = room(0, owner)
        choices = [(bit_of(named, near) == 0) & core_room]
        for m in range(1, len(RELAY_MASKS)):
            choices.append((bit_of(named, owner ^ RELAY_MASKS[m]) == 0) & room(m, owner))
        swap = core_room & (bit_of(direct_ref[s], near) == 1)
        for m in range(1, len(RELAY_MASKS)):
            choices.append(swap & (bit_of(named, near ^ RELAY_MASKS[m]) == 0) & room(m, near))
        choice = jnp.int32(len(choices))
        for c in reversed(range(len(choices))):
            choice = jnp.where(choices[c], jnp.int32(c), choice)
        for c in range(len(choices)):
            m = c if c < len(RELAY_MASKS) else c - len(RELAY_MASKS) + 1

            @pl.when(choice == c)
            def _():
                target = owner if c < len(RELAY_MASKS) else near
                via = target ^ RELAY_MASKS[m]
                count = used_ref[m * owners + target]
                used_ref[m * owners + target] = count + 1
                named_ref[s] = named | lax.shift_left(jnp.int32(1), via)
                record(s, via, target, 1 if c < len(RELAY_MASKS) else 0, m, offsets[m] + count)
                if c >= len(RELAY_MASKS):
                    direct_ref[s] = direct_ref[s] ^ lax.shift_left(jnp.int32(1), near)
                    count = used_ref[owner]
                    used_ref[owner] = count + 1
                    record(s, near, owner, 1, 0, offsets[0] + count)

        return failed | (choice == len(choices)).astype(jnp.int32)

    failed = lax.fori_loop(0, seconds, route, jnp.int32(0))
    route_ref[head] = failed

    @pl.when(failed == 1)
    def _():
        def undo(s, _):
            route_ref[s] = s
            route_ref[owners + s] = owners + relays + s
            place_ref[s] = s
            return 0

        lax.fori_loop(0, owners, undo, 0)
        route_ref[head + 1] = 0

    def send(k, _):
        rank = kept_ref[k]

        @pl.when(rank >= 0)
        def _():
            owner = dest_ref[me * blocks_dev + k]
            late = (rank == 1) & (failed == 1)

            @pl.when(late)
            def _():
                pltpu.make_async_copy(blocks_ref.at[k], late_ref.at[owner], sem).start()

            @pl.when(jnp.logical_not(late))
            def _():
                slot = place_ref[rank * owners + owner]
                pltpu.make_async_copy(blocks_ref.at[k], out_ref.at[slot], sem).start()

        return 0

    lax.fori_loop(0, blocks_dev, send, 0)
    pltpu.make_async_copy(blocks_ref, out_ref.at[pl.ds(0, blocks_dev)], sem).wait()


def pack(me, dest, blocks, owners):
    blocks_dev = blocks.shape[0]
    smem = pl.BlockSpec(memory_space=pltpu.SMEM)
    hbm = pl.BlockSpec(memory_space=pl.ANY)
    slots = jax.ShapeDtypeStruct((owners,) + blocks.shape[1:], blocks.dtype)
    relays = relay_offsets()[1]
    return pl.pallas_call(
        functools.partial(pack_kernel, owners, blocks_dev),
        out_shape=(slots, slots, jax.ShapeDtypeStruct((2 * owners + 2 + relays,), jnp.int32)),
        in_specs=[smem, smem, pl.BlockSpec(memory_space=pltpu.VMEM)],
        out_specs=(hbm, hbm, smem),
        scratch_shapes=[
            pltpu.SMEM((owners,), jnp.int32),
            pltpu.SMEM((owners,), jnp.int32),
            pltpu.SMEM((owners * blocks_dev,), jnp.int32),
            pltpu.SMEM((len(RELAY_MASKS) * owners,), jnp.int32),
            pltpu.SMEM((2 * owners,), jnp.int32),
            pltpu.SMEM((owners,), jnp.int32),
            pltpu.SMEM((blocks_dev,), jnp.int32),
            pltpu.SemaphoreType.DMA,
        ],
        name="pack",
    )(me, dest, blocks)


def forward_kernel(owners, route_ref, recv_ref, *refs):
    relay_refs, stage_ref, sem = refs[: len(RELAY_MASKS)], refs[-2], refs[-1]
    offsets, relays = relay_offsets()
    head = 2 * owners
    count = route_ref[head + 1]

    def take(i, _):
        slot = lax.shift_right_logical(route_ref[head + 2 + i], RELAY_SPAN_BITS)
        pltpu.make_async_copy(recv_ref.at[slot], stage_ref.at[i], sem).start()
        return 0

    def give(i, _):
        place = route_ref[head + 2 + i] & (RELAY_SPAN - 1)
        for ref, offset, cap in zip(relay_refs, offsets, RELAY_CAPS):
            @pl.when((place >= offset) & (place < offset + cap))
            def _():
                pltpu.make_async_copy(stage_ref.at[i], ref.at[place - offset], sem).start()

        return 0

    def wait(i, _):
        pltpu.make_async_copy(recv_ref.at[0], stage_ref.at[0], sem).wait()
        return 0

    lax.fori_loop(0, count, take, 0)
    lax.fori_loop(0, count, wait, 0)
    lax.fori_loop(0, count, give, 0)
    lax.fori_loop(0, count, wait, 0)


def forward(route, recv):
    owners = recv.shape[0]
    hbm = pl.BlockSpec(memory_space=pl.ANY)
    block = recv.shape[1:]
    return pl.pallas_call(
        functools.partial(forward_kernel, owners),
        out_shape=tuple(jax.ShapeDtypeStruct((cap,) + block, recv.dtype) for cap in RELAY_CAPS),
        in_specs=[pl.BlockSpec(memory_space=pltpu.SMEM), hbm],
        out_specs=(hbm,) * len(RELAY_CAPS),
        scratch_shapes=[pltpu.VMEM((relay_offsets()[1],) + block, recv.dtype), pltpu.SemaphoreType.DMA],
        name="forward",
    )(route, recv)


def plan_kernel(owners, blocks_dev, ao_blocks, me_ref, dest_ref, row_ref, col_ref, route_ref, table_ref):
    me = me_ref[0]
    most = owners * CAP
    cells = ao_blocks * ao_blocks

    def clear(c, _):
        table_ref[c] = most
        return 0

    lax.fori_loop(0, cells, clear, 0)
    tail = cells + 2 * most + 1
    for r in range(ao_blocks + groups_of(ao_blocks)):
        table_ref[tail + r] = 0

    def source(s, total):
        def block(k, carry):
            rank, total = carry
            index = s * blocks_dev + k
            mine = dest_ref[index] == me

            @pl.when(mine)
            def _():
                row = row_ref[index]
                cell = row * ao_blocks + col_ref[index]
                table_ref[cells + total] = table_ref[cell]
                table_ref[cell] = total
                place = route_ref[rank * owners + s]
                table_ref[cells + most + total] = place | lax.shift_left(row, PLACE_BITS)
                late = (place >= owners).astype(jnp.int32)
                table_ref[tail + row] += 1 - late
                table_ref[tail + ao_blocks + lax.shift_right_logical(cell, GROUP_BITS)] += late

            step = mine.astype(jnp.int32)
            return rank + step, total + step

        return lax.fori_loop(0, blocks_dev, block, (jnp.int32(0), total))[1]

    table_ref[cells + 2 * most] = lax.fori_loop(0, owners, source, jnp.int32(0))


def plan(me, dest, row, col, route, owners, blocks_dev, ao_blocks):
    smem = pl.BlockSpec(memory_space=pltpu.SMEM)
    most = owners * CAP
    return pl.pallas_call(
        functools.partial(plan_kernel, owners, blocks_dev, ao_blocks),
        out_shape=jax.ShapeDtypeStruct((ao_blocks * ao_blocks + 2 * most + 1 + ao_blocks + groups_of(ao_blocks),), jnp.int32),
        in_specs=[smem] * 5,
        out_specs=smem,
        name="plan",
    )(me, dest, row, col, route)


def merge_cells(most, ao_blocks, first_cell, table_ref, held, total):
    cells = ao_blocks * ao_blocks

    def merge(c, _):
        first = table_ref[c]

        @pl.when(first < most)
        def _():
            second = table_ref[cells + first]

            @pl.when(second < most)
            def _():
                total[...] = held[first].astype(jnp.float32)

                def add(slot):
                    total[...] += held[slot].astype(jnp.float32)
                    return table_ref[cells + slot]

                lax.while_loop(lambda slot: slot < most, add, second)
                held[first] = total[...].astype(held.dtype)

        return 0

    lax.fori_loop(first_cell, first_cell + (1 << GROUP_BITS), merge, 0)


def place_group(first_cell, r, tile, lanes, table_ref, shuffle, held, dense, work):
    per_tile = LANES // BA
    sources = [table_ref[first_cell + j] for j in range(per_tile)]
    x = jnp.concatenate(
        [
            jnp.concatenate([held[s, :, hi * LANES : (hi + 1) * LANES] for s in sources], axis=1)
            for hi in range(BA // per_tile)
        ],
        axis=0,
    )
    y = jnp.dot(x, shuffle, preferred_element_type=jnp.float32)
    for hi in range(BA // per_tile):
        for j in range(per_tile):
            mu = r * BA + hi * per_tile + j
            part = y[hi * BR : (hi + 1) * BR, j * LANES : (j + 1) * LANES]
            work[tile, pl.ds(mu * PITCH, BR), :] = part
            dense[mu, :, lanes] = part.astype(jnp.bfloat16)


def assemble_kernel(most, ao_blocks, table_ref, shuffle_ref, recv_ref, held, dense, work, total, sem):
    cells = ao_blocks * ao_blocks
    per_tile = LANES // BA
    tiles = ao_blocks // per_tile
    tail = cells + 2 * most + 1

    def fetch(i, _):
        entry = table_ref[cells + most + i]
        place = entry & ((1 << PLACE_BITS) - 1)
        row = lax.shift_right_logical(entry, PLACE_BITS)

        @pl.when(place < recv_ref.shape[0])
        def _():
            pltpu.make_async_copy(recv_ref.at[place], held.at[i], sem.at[row]).start()

        return 0

    lax.fori_loop(0, table_ref[cells + 2 * most], fetch, 0)
    held[most] = jnp.zeros(held.shape[1:], held.dtype)
    shuffle = shuffle_ref[...]

    def row(r, _):
        def arrive(i, _):
            pltpu.make_async_copy(recv_ref.at[0], held.at[0], sem.at[r]).wait()
            return 0

        lax.fori_loop(0, table_ref[tail + r], arrive, 0)
        for tile in range(tiles):
            first_cell = r * ao_blocks + tile * per_tile

            @pl.when(table_ref[tail + ao_blocks + r * tiles + tile] == 0)
            def _():
                merge_cells(most, ao_blocks, first_cell, table_ref, held, total)
                lanes = slice(tile * LANES, (tile + 1) * LANES)
                place_group(first_cell, r, tile, lanes, table_ref, shuffle, held, dense, work)

        return 0

    lax.fori_loop(0, ao_blocks, row, 0)


def assemble(table, shuffle, recv, most, ao_blocks):
    width = ao_blocks * BA
    vmem = pl.BlockSpec(memory_space=pltpu.VMEM)
    return pl.pallas_call(
        functools.partial(assemble_kernel, most, ao_blocks),
        out_shape=(
            pltpu.VMEM((most + 1, BR, BA * BA), jnp.bfloat16),
            pltpu.VMEM((width, BR, width), jnp.bfloat16),
            pltpu.VMEM((width // LANES, width * PITCH, LANES), jnp.float32),
        ),
        in_specs=[pl.BlockSpec(memory_space=pltpu.SMEM), vmem, pl.BlockSpec(memory_space=pl.ANY)],
        out_specs=(vmem, vmem, vmem),
        scratch_shapes=[pltpu.VMEM((BR, BA * BA), jnp.float32), pltpu.SemaphoreType.DMA((ao_blocks,))],
        compiler_params=pltpu.CompilerParams(vmem_limit_bytes=SCOPED),
        cost_estimate=pl.CostEstimate(flops=1 << 32, bytes_accessed=1 << 24, transcendentals=0),
        name="assemble",
    )(table, shuffle, recv)


def slab_kernel(most, ao_blocks, table_ref, occ_ref, virt_ref, shuffle_ref, *refs):
    late_refs = refs[:-9]
    held, dense, work = refs[-6:-3]
    out_ref, total, sem = refs[-3:]
    width = ao_blocks * BA
    cells = ao_blocks * ao_blocks
    per_tile = LANES // BA
    tiles = width // LANES
    tail = cells + 2 * most + 1
    slots = most // CAP

    def fetch(i, late):
        place = table_ref[cells + most + i] & ((1 << PLACE_BITS) - 1)

        @pl.when(place >= slots)
        def _():
            offset = slots
            for ref in late_refs:
                @pl.when((place >= offset) & (place < offset + ref.shape[0]))
                def _():
                    pltpu.make_async_copy(ref.at[place - offset], held.at[i], sem).start()

                offset += ref.shape[0]

        return late + (place >= slots).astype(jnp.int32)

    late = lax.fori_loop(0, table_ref[cells + 2 * most], fetch, jnp.int32(0))

    def arrive(i, _):
        pltpu.make_async_copy(late_refs[0].at[0], held.at[0], sem).wait()
        return 0

    lax.fori_loop(0, late, arrive, 0)

    def place(step, _):
        @pl.when(table_ref[tail + ao_blocks + step] > 0)
        def _():
            r, tile = step // tiles, step % tiles
            first_cell = step * per_tile
            merge_cells(most, ao_blocks, first_cell, table_ref, held, total)
            lanes = pl.ds(pl.multiple_of(tile * LANES, LANES), LANES)
            place_group(first_cell, r, tile, lanes, table_ref, shuffle_ref[...], held, dense, work)

        return 0

    lax.fori_loop(0, groups_of(ao_blocks), place, 0)

    occ_t = occ_ref[...].astype(jnp.float32).T.astype(jnp.bfloat16)
    virt = virt_ref[...]

    def transform(i, _):
        for j in range(16):
            rows = pl.ds(i * 16 + j, width, stride=PITCH)
            part = jnp.concatenate([work[t, rows, :] for t in range(tiles)], axis=1).astype(jnp.bfloat16)
            half = jnp.dot(occ_t, part, preferred_element_type=jnp.float32).astype(jnp.bfloat16)
            both = jnp.dot(half, virt, preferred_element_type=jnp.float32)
            for t in range(tiles):
                work[t, rows, :] = both[:, t * LANES : (t + 1) * LANES]
        return 0

    lax.fori_loop(0, BR // 16, transform, 0)

    def contract(i, acc):
        left, right = [], []
        for j in range(32):
            mu = i * 32 + j
            left += [work[t, pl.ds(mu * PITCH, BR), :] for t in range(tiles)]
            right.append(dense[mu])
        return acc + lax.dot_general(
            jnp.concatenate(left, axis=1).astype(jnp.bfloat16),
            jnp.concatenate(right, axis=1),
            (((1,), (1,)), ((), ())),
            preferred_element_type=jnp.float32,
        )

    out_ref[...] = lax.fori_loop(0, width // 32, contract, jnp.zeros((BR, BR), jnp.float32))


def lane_shuffle():
    side = LANES // BA
    lane, to = (lax.broadcasted_iota(jnp.int32, (side * LANES, side * LANES), axis) for axis in (0, 1))
    target = ((lane >> 5) & (side - 1)) * LANES + (lane >> 7) * BA + (lane & (BA - 1))
    return (to == target).astype(jnp.bfloat16)


def slab(table, occ, virt, shuffle, late, assembled, most, ao_blocks):
    smem = pl.BlockSpec(memory_space=pltpu.SMEM)
    vmem = pl.BlockSpec(memory_space=pltpu.VMEM)
    first = 4 + len(late)
    return pl.pallas_call(
        functools.partial(slab_kernel, most, ao_blocks),
        out_shape=tuple(pltpu.VMEM(a.shape, a.dtype) for a in assembled)
        + (jax.ShapeDtypeStruct((BR, BR), jnp.float32),),
        in_specs=[smem, vmem, vmem, vmem] + [pl.BlockSpec(memory_space=pltpu.HBM)] * len(late) + [vmem] * 3,
        out_specs=(vmem,) * 4,
        input_output_aliases={first + i: i for i in range(3)},
        scratch_shapes=[pltpu.VMEM((BR, BA * BA), jnp.float32), pltpu.SemaphoreType.DMA],
        compiler_params=pltpu.CompilerParams(vmem_limit_bytes=SCOPED),
        name="slab",
    )(table, occ, virt, shuffle, *late, *assembled)[3]


def body(
    three_center, block_dest, block_row, block_col, occ_density, virt_density, occ_mask, virt_mask
):
    owners = lax.axis_size(("ri", "pair"))
    blocks_dev = three_center.shape[0]
    ao_blocks = occ_mask.shape[1]
    width = occ_density.shape[1]
    me = lax.axis_index(("ri", "pair")).astype(jnp.int32).reshape(1)
    dest = block_dest.reshape(-1)
    outgoing, late, route = pack(me, dest, three_center, owners)
    group = ("ri", "pair")

    def exchange(slots):
        return lax.all_to_all(slots, group, split_axis=0, concat_axis=0, tiled=True)

    incoming = exchange(outgoing)
    local = jnp.concatenate(
        [
            occ_density * expand(occ_mask, BA).astype(jnp.bfloat16),
            virt_density * expand(virt_mask, BA).astype(jnp.bfloat16),
        ],
        axis=1,
    )
    need_late = jnp.broadcast_to(route[2 * owners].astype(jnp.bfloat16), (8, 2 * width))
    height = local.shape[0]
    gathered = lax.all_gather(jnp.concatenate([local, need_late], axis=0), "orb", axis=0, tiled=True)
    gathered = gathered.reshape(-1, height + 8, 2 * width)
    whole = gathered[:, :height].reshape(width, 2 * width)
    any_late = jnp.max(gathered[:, height, 0]) > 0
    table = plan(me, dest, block_row, block_col, route, owners, blocks_dev, ao_blocks)
    route, table, occ, virt, shuffle, any_late = lax.optimization_barrier(
        (route, table, whole[:, :width], whole[:, width:], lane_shuffle(), any_late)
    )
    incoming, late = lax.optimization_barrier((incoming, late))
    late = lax.cond(any_late, exchange, lambda slots: slots, late)
    relayed = [
        lax.ppermute(part, group, [(i, i ^ mask) for i in range(owners)])
        for part, mask in zip(forward(route, incoming), RELAY_MASKS)
    ]
    assembled = assemble(table, shuffle, incoming, owners * CAP, ao_blocks)
    return slab(table, occ, virt, shuffle, [*relayed, late], assembled, owners * CAP, ao_blocks)


def solution(mesh):
    placed = (
        P(("orb", "ri", "pair"), None, None),
        P("orb", None),
        P("orb"),
        P("orb"),
        P("orb", None),
        P("orb", None),
        P("orb", None),
        P("orb", None),
    )
    return jax.shard_map(
        body, mesh=mesh, in_specs=placed, out_specs=P(("orb", "ri", "pair"), None), check_vma=False
    )
```

```python
import functools

import jax
import jax.numpy as jnp
from jax import lax
from jax.experimental import pallas as pl
from jax.experimental.pallas import tpu as pltpu
from jax.sharding import PartitionSpec as P

BR = 64
BA = 32
CAP = 2
LANES = 128
PITCH = BR + 1
OWNER_BITS = 5
RELAY_SPAN_BITS = 6
RELAY_SPAN = 1 << RELAY_SPAN_BITS
RELAY_MASKS = (4, 1, 3, 8, 24)
RELAY_CAPS = (12, 2, 2, 2, 2)
NEAR_SHIFT = 4
NEAR_LOW = 0x0F0F0F0F
PLACE_BITS = 7
GROUP_BITS = 2
SCOPED = 12 * 1024 * 1024


def expand(mask_blocks, block_width):
    return jnp.repeat(jnp.repeat(mask_blocks, block_width, axis=0), block_width, axis=1)


def relay_offsets():
    offsets, total = [], 0
    for cap in RELAY_CAPS:
        offsets.append(total)
        total += cap
    return offsets, total


def groups_of(ao_blocks):
    return ao_blocks * ao_blocks >> GROUP_BITS


def bit_of(word, index):
    return lax.shift_right_logical(word, index) & 1


def pack_kernel(
    owners, blocks_dev, me_ref, dest_ref, blocks_ref, out_ref, late_ref, route_ref,
    named_ref, direct_ref, second_ref, used_ref, place_ref, rank_ref, kept_ref, sem,
):
    me = me_ref[0]
    offsets, relays = relay_offsets()

    def tally(s):
        bits = [lax.shift_left(jnp.int32(1), dest_ref[s * blocks_dev + k]) for k in range(blocks_dev)]
        named = functools.reduce(lax.bitwise_or, bits)
        return named, functools.reduce(lax.add, bits) - named

    def clear(o, _):
        rank_ref[o] = 0
        return 0

    lax.fori_loop(0, owners, clear, 0)
    twice = tally(me)[1]
    low = jnp.int32(NEAR_LOW)
    near_twice = lax.shift_left(twice & low, NEAR_SHIFT) | (lax.shift_right_logical(twice, NEAR_SHIFT) & low)

    def send_early(k, _):
        owner = dest_ref[me * blocks_dev + k]
        rank = rank_ref[owner]
        rank_ref[owner] = rank + 1
        early = (rank == 0) & (bit_of(near_twice, owner) == 0)
        kept_ref[k] = jnp.where(early, -1, rank)

        @pl.when(early)
        def _():
            pltpu.make_async_copy(blocks_ref.at[k], out_ref.at[owner], sem).start()

        return 0

    lax.fori_loop(0, blocks_dev, send_early, 0)

    def list_seconds(s, total):
        seen = jnp.int32(0)
        for k in range(blocks_dev):
            owner = dest_ref[s * blocks_dev + k]
            second_ref[total] = s * owners + owner
            total = total + bit_of(seen, owner)
            seen = seen | lax.shift_left(jnp.int32(1), owner)
        return total

    def start(s, total):
        named, doubled = tally(s)
        total = lax.cond(doubled != 0, lambda: list_seconds(s, total), lambda: total)
        named_ref[s] = named
        direct_ref[s] = named
        route_ref[s] = s
        route_ref[owners + s] = owners + relays + s
        place_ref[s] = s
        for m in range(len(RELAY_MASKS)):
            used_ref[m * owners + s] = 0
        return total

    seconds = lax.fori_loop(0, owners, start, jnp.int32(0))
    head = 2 * owners
    route_ref[head + 1] = 0

    def record(s, via, owner, rank, mask_index, place):
        @pl.when(owner == me)
        def _():
            route_ref[rank * owners + s] = owners + place

        @pl.when(via == me)
        def _():
            count = route_ref[head + 1]
            route_ref[head + 2 + count] = s * RELAY_SPAN + place
            route_ref[head + 1] = count + 1

        @pl.when(s == me)
        def _():
            place_ref[rank * owners + owner] = via

    def room(mask_index, owner):
        return used_ref[mask_index * owners + owner] < RELAY_CAPS[mask_index]

    def route(e, failed):
        pair = second_ref[e]
        s, owner = lax.shift_right_logical(pair, OWNER_BITS), pair & (owners - 1)
        named = named_ref[s]
        near = owner ^ RELAY_MASKS[0]
        core_room = room(0, owner)
        choices = [(bit_of(named, near) == 0) & core_room]
        for m in range(1, len(RELAY_MASKS)):
            choices.append((bit_of(named, owner ^ RELAY_MASKS[m]) == 0) & room(m, owner))
        swap = core_room & (bit_of(direct_ref[s], near) == 1)
        for m in range(1, len(RELAY_MASKS)):
            choices.append(swap & (bit_of(named, near ^ RELAY_MASKS[m]) == 0) & room(m, near))
        choice = jnp.int32(len(choices))
        for c in reversed(range(len(choices))):
            choice = jnp.where(choices[c], jnp.int32(c), choice)
        for c in range(len(choices)):
            m = c if c < len(RELAY_MASKS) else c - len(RELAY_MASKS) + 1

            @pl.when(choice == c)
            def _():
                target = owner if c < len(RELAY_MASKS) else near
                via = target ^ RELAY_MASKS[m]
                count = used_ref[m * owners + target]
                used_ref[m * owners + target] = count + 1
                named_ref[s] = named | lax.shift_left(jnp.int32(1), via)
                record(s, via, target, 1 if c < len(RELAY_MASKS) else 0, m, offsets[m] + count)
                if c >= len(RELAY_MASKS):
                    direct_ref[s] = direct_ref[s] ^ lax.shift_left(jnp.int32(1), near)
                    count = used_ref[owner]
                    used_ref[owner] = count + 1
                    record(s, near, owner, 1, 0, offsets[0] + count)

        return failed | (choice == len(choices)).astype(jnp.int32)

    failed = lax.fori_loop(0, seconds, route, jnp.int32(0))
    route_ref[head] = failed

    @pl.when(failed == 1)
    def _():
        def undo(s, _):
            route_ref[s] = s
            route_ref[owners + s] = owners + relays + s
            place_ref[s] = s
            return 0

        lax.fori_loop(0, owners, undo, 0)
        route_ref[head + 1] = 0

    def send(k, _):
        rank = kept_ref[k]

        @pl.when(rank >= 0)
        def _():
            owner = dest_ref[me * blocks_dev + k]
            late = (rank == 1) & (failed == 1)

            @pl.when(late)
            def _():
                pltpu.make_async_copy(blocks_ref.at[k], late_ref.at[owner], sem).start()

            @pl.when(jnp.logical_not(late))
            def _():
                slot = place_ref[rank * owners + owner]
                pltpu.make_async_copy(blocks_ref.at[k], out_ref.at[slot], sem).start()

        return 0

    lax.fori_loop(0, blocks_dev, send, 0)
    pltpu.make_async_copy(blocks_ref, out_ref.at[pl.ds(0, blocks_dev)], sem).wait()


def pack(me, dest, blocks, owners):
    blocks_dev = blocks.shape[0]
    smem = pl.BlockSpec(memory_space=pltpu.SMEM)
    hbm = pl.BlockSpec(memory_space=pl.ANY)
    slots = jax.ShapeDtypeStruct((owners,) + blocks.shape[1:], blocks.dtype)
    relays = relay_offsets()[1]
    return pl.pallas_call(
        functools.partial(pack_kernel, owners, blocks_dev),
        out_shape=(slots, slots, jax.ShapeDtypeStruct((2 * owners + 2 + relays,), jnp.int32)),
        in_specs=[smem, smem, pl.BlockSpec(memory_space=pltpu.VMEM)],
        out_specs=(hbm, hbm, smem),
        scratch_shapes=[
            pltpu.SMEM((owners,), jnp.int32),
            pltpu.SMEM((owners,), jnp.int32),
            pltpu.SMEM((owners * blocks_dev,), jnp.int32),
            pltpu.SMEM((len(RELAY_MASKS) * owners,), jnp.int32),
            pltpu.SMEM((2 * owners,), jnp.int32),
            pltpu.SMEM((owners,), jnp.int32),
            pltpu.SMEM((blocks_dev,), jnp.int32),
            pltpu.SemaphoreType.DMA,
        ],
        name="pack",
    )(me, dest, blocks)


def forward_kernel(owners, route_ref, recv_ref, *refs):
    relay_refs, stage_ref, sem = refs[: len(RELAY_MASKS)], refs[-2], refs[-1]
    offsets, relays = relay_offsets()
    head = 2 * owners
    count = route_ref[head + 1]

    def take(i, _):
        slot = lax.shift_right_logical(route_ref[head + 2 + i], RELAY_SPAN_BITS)
        pltpu.make_async_copy(recv_ref.at[slot], stage_ref.at[i], sem).start()
        return 0

    def give(i, _):
        place = route_ref[head + 2 + i] & (RELAY_SPAN - 1)
        for ref, offset, cap in zip(relay_refs, offsets, RELAY_CAPS):
            @pl.when((place >= offset) & (place < offset + cap))
            def _():
                pltpu.make_async_copy(stage_ref.at[i], ref.at[place - offset], sem).start()

        return 0

    def wait(i, _):
        pltpu.make_async_copy(recv_ref.at[0], stage_ref.at[0], sem).wait()
        return 0

    lax.fori_loop(0, count, take, 0)
    lax.fori_loop(0, count, wait, 0)
    lax.fori_loop(0, count, give, 0)
    lax.fori_loop(0, count, wait, 0)


def forward(route, recv):
    owners = recv.shape[0]
    hbm = pl.BlockSpec(memory_space=pl.ANY)
    block = recv.shape[1:]
    return pl.pallas_call(
        functools.partial(forward_kernel, owners),
        out_shape=tuple(jax.ShapeDtypeStruct((cap,) + block, recv.dtype) for cap in RELAY_CAPS),
        in_specs=[pl.BlockSpec(memory_space=pltpu.SMEM), hbm],
        out_specs=(hbm,) * len(RELAY_CAPS),
        scratch_shapes=[pltpu.VMEM((relay_offsets()[1],) + block, recv.dtype), pltpu.SemaphoreType.DMA],
        name="forward",
    )(route, recv)


def plan_kernel(
    owners, blocks_dev, ao_blocks, me_ref, dest_ref, row_ref, col_ref, route_ref, table_ref, mine_ref
):
    me = me_ref[0]
    most = owners * CAP
    cells = ao_blocks * ao_blocks

    def clear(c, _):
        table_ref[c] = most
        return 0

    lax.fori_loop(0, cells, clear, 0)
    tail = cells + 2 * most + 1
    for r in range(ao_blocks + groups_of(ao_blocks)):
        table_ref[tail + r] = 0

    def scan(s, total):
        for k in range(blocks_dev):
            index = s * blocks_dev + k
            mine_ref[total] = index
            total = total + (dest_ref[index] == me).astype(jnp.int32)
        return total

    count = lax.fori_loop(0, owners, scan, jnp.int32(0))
    table_ref[cells + 2 * most] = count

    def enter(i, before):
        index = mine_ref[i]
        s = lax.div(index, blocks_dev)
        row = row_ref[index]
        cell = row * ao_blocks + col_ref[index]
        table_ref[cells + i] = table_ref[cell]
        table_ref[cell] = i
        place = route_ref[jnp.where(s == before, owners, 0) + s]
        table_ref[cells + most + i] = place | lax.shift_left(row, PLACE_BITS)
        late = (place >= owners).astype(jnp.int32)
        table_ref[tail + row] += 1 - late
        table_ref[tail + ao_blocks + lax.shift_right_logical(cell, GROUP_BITS)] += late
        return s

    lax.fori_loop(0, count, enter, jnp.int32(-1))


def plan(me, dest, row, col, route, owners, blocks_dev, ao_blocks):
    smem = pl.BlockSpec(memory_space=pltpu.SMEM)
    most = owners * CAP
    return pl.pallas_call(
        functools.partial(plan_kernel, owners, blocks_dev, ao_blocks),
        out_shape=jax.ShapeDtypeStruct((ao_blocks * ao_blocks + 2 * most + 1 + ao_blocks + groups_of(ao_blocks),), jnp.int32),
        in_specs=[smem] * 5,
        out_specs=smem,
        scratch_shapes=[pltpu.SMEM((most + 1,), jnp.int32)],
        name="plan",
    )(me, dest, row, col, route)


def merge_cells(most, ao_blocks, first_cell, table_ref, held, total):
    cells = ao_blocks * ao_blocks

    def merge(c, _):
        first = table_ref[c]

        @pl.when(first < most)
        def _():
            second = table_ref[cells + first]

            @pl.when(second < most)
            def _():
                total[...] = held[first].astype(jnp.float32)

                def add(slot):
                    total[...] += held[slot].astype(jnp.float32)
                    return table_ref[cells + slot]

                lax.while_loop(lambda slot: slot < most, add, second)
                held[first] = total[...].astype(held.dtype)

        return 0

    lax.fori_loop(first_cell, first_cell + (1 << GROUP_BITS), merge, 0)


def pair_shuffle():
    lane, to = (lax.broadcasted_iota(jnp.int32, (2 * LANES, 2 * LANES), axis) for axis in (0, 1))
    target = ((lane & 32) << 2) | (lane & 64) | ((lane & 128) >> 2) | (lane & 31)
    return (to == target).astype(jnp.float32).astype(jnp.bfloat16)


def place_group(first_cell, r, tile, lanes, table_ref, shuffle, held, dense, work):
    high = BA // 4
    x = []
    for j in range(4):
        s = table_ref[first_cell + j]
        x.append(jnp.concatenate([held[s, :, hi * LANES : (hi + 1) * LANES] for hi in range(high)], axis=0))
    low = lax.broadcasted_iota(jnp.int32, x[0].shape, 1) < LANES // 2
    z = [None] * 4
    for a in (0, 1):
        z[a] = jnp.where(low, x[a], pltpu.roll(x[a + 2], LANES // 2, 1))
        z[a + 2] = jnp.where(low, pltpu.roll(x[a], LANES // 2, 1), x[a + 2])
    y = [
        jnp.dot(jnp.concatenate(z[a : a + 2], axis=1), shuffle, preferred_element_type=jnp.float32)
        for a in (0, 2)
    ]
    for hi in range(high):
        for j in range(4):
            mu = r * BA + hi * 4 + j
            part = y[j // 2][hi * BR : (hi + 1) * BR, (j % 2) * LANES : (j % 2 + 1) * LANES]
            work[tile, pl.ds(mu * PITCH, BR), :] = part
            dense[mu, :, lanes] = part.astype(jnp.bfloat16)


def assemble_kernel(most, ao_blocks, table_ref, recv_ref, held, dense, work, total, sem):
    cells = ao_blocks * ao_blocks
    per_tile = LANES // BA
    tiles = ao_blocks // per_tile
    tail = cells + 2 * most + 1

    def fetch(i, _):
        entry = table_ref[cells + most + i]
        place = entry & ((1 << PLACE_BITS) - 1)
        row = lax.shift_right_logical(entry, PLACE_BITS)

        @pl.when(place < recv_ref.shape[0])
        def _():
            pltpu.make_async_copy(recv_ref.at[place], held.at[i], sem.at[row]).start()

        return 0

    lax.fori_loop(0, table_ref[cells + 2 * most], fetch, 0)
    held[most] = jnp.zeros(held.shape[1:], held.dtype)
    shuffle = pair_shuffle()

    def row(r, _):
        def arrive(i, _):
            pltpu.make_async_copy(recv_ref.at[0], held.at[0], sem.at[r]).wait()
            return 0

        lax.fori_loop(0, table_ref[tail + r], arrive, 0)
        for tile in range(tiles):
            first_cell = r * ao_blocks + tile * per_tile

            @pl.when(table_ref[tail + ao_blocks + r * tiles + tile] == 0)
            def _():
                merge_cells(most, ao_blocks, first_cell, table_ref, held, total)
                lanes = slice(tile * LANES, (tile + 1) * LANES)
                place_group(first_cell, r, tile, lanes, table_ref, shuffle, held, dense, work)

        return 0

    lax.fori_loop(0, ao_blocks, row, 0)


def assemble(table, recv, most, ao_blocks):
    width = ao_blocks * BA
    vmem = pl.BlockSpec(memory_space=pltpu.VMEM)
    return pl.pallas_call(
        functools.partial(assemble_kernel, most, ao_blocks),
        out_shape=(
            pltpu.VMEM((most + 1, BR, BA * BA), jnp.bfloat16),
            pltpu.VMEM((width, BR, width), jnp.bfloat16),
            pltpu.VMEM((width // LANES, width * PITCH, LANES), jnp.float32),
        ),
        in_specs=[pl.BlockSpec(memory_space=pltpu.SMEM), pl.BlockSpec(memory_space=pl.ANY)],
        out_specs=(vmem, vmem, vmem),
        scratch_shapes=[pltpu.VMEM((BR, BA * BA), jnp.float32), pltpu.SemaphoreType.DMA((ao_blocks,))],
        compiler_params=pltpu.CompilerParams(vmem_limit_bytes=SCOPED),
        cost_estimate=pl.CostEstimate(flops=1 << 32, bytes_accessed=1 << 24, transcendentals=0),
        name="assemble",
    )(table, recv)


def slab_kernel(most, ao_blocks, table_ref, occ_ref, virt_ref, *refs):
    late_refs = refs[:-9]
    held, dense, work = refs[-6:-3]
    out_ref, total, sem = refs[-3:]
    width = ao_blocks * BA
    cells = ao_blocks * ao_blocks
    per_tile = LANES // BA
    tiles = width // LANES
    tail = cells + 2 * most + 1
    slots = most // CAP

    def fetch(i, late):
        place = table_ref[cells + most + i] & ((1 << PLACE_BITS) - 1)

        @pl.when(place >= slots)
        def _():
            offset = slots
            for ref in late_refs:
                @pl.when((place >= offset) & (place < offset + ref.shape[0]))
                def _():
                    pltpu.make_async_copy(ref.at[place - offset], held.at[i], sem).start()

                offset += ref.shape[0]

        return late + (place >= slots).astype(jnp.int32)

    late = lax.fori_loop(0, table_ref[cells + 2 * most], fetch, jnp.int32(0))

    def arrive(i, _):
        pltpu.make_async_copy(late_refs[0].at[0], held.at[0], sem).wait()
        return 0

    lax.fori_loop(0, late, arrive, 0)

    shuffle = pair_shuffle()

    def place(step, _):
        @pl.when(table_ref[tail + ao_blocks + step] > 0)
        def _():
            r, tile = step // tiles, step % tiles
            first_cell = step * per_tile
            merge_cells(most, ao_blocks, first_cell, table_ref, held, total)
            lanes = pl.ds(pl.multiple_of(tile * LANES, LANES), LANES)
            place_group(first_cell, r, tile, lanes, table_ref, shuffle, held, dense, work)

        return 0

    lax.fori_loop(0, groups_of(ao_blocks), place, 0)

    occ_t = occ_ref[...].astype(jnp.float32).T.astype(jnp.bfloat16)
    virt = virt_ref[...]

    def transform(i, _):
        for j in range(16):
            rows = pl.ds(i * 16 + j, width, stride=PITCH)
            part = jnp.concatenate([work[t, rows, :] for t in range(tiles)], axis=1).astype(jnp.bfloat16)
            half = jnp.dot(occ_t, part, preferred_element_type=jnp.float32).astype(jnp.bfloat16)
            both = jnp.dot(half, virt, preferred_element_type=jnp.float32)
            for t in range(tiles):
                work[t, rows, :] = both[:, t * LANES : (t + 1) * LANES]
        return 0

    lax.fori_loop(0, BR // 16, transform, 0)

    def contract(i, acc):
        left, right = [], []
        for j in range(32):
            mu = i * 32 + j
            left += [work[t, pl.ds(mu * PITCH, BR), :] for t in range(tiles)]
            right.append(dense[mu])
        return acc + lax.dot_general(
            jnp.concatenate(left, axis=1).astype(jnp.bfloat16),
            jnp.concatenate(right, axis=1),
            (((1,), (1,)), ((), ())),
            preferred_element_type=jnp.float32,
        )

    out_ref[...] = lax.fori_loop(0, width // 32, contract, jnp.zeros((BR, BR), jnp.float32))


def slab(table, occ, virt, late, assembled, most, ao_blocks):
    smem = pl.BlockSpec(memory_space=pltpu.SMEM)
    vmem = pl.BlockSpec(memory_space=pltpu.VMEM)
    first = 3 + len(late)
    return pl.pallas_call(
        functools.partial(slab_kernel, most, ao_blocks),
        out_shape=tuple(pltpu.VMEM(a.shape, a.dtype) for a in assembled)
        + (jax.ShapeDtypeStruct((BR, BR), jnp.float32),),
        in_specs=[smem, vmem, vmem] + [pl.BlockSpec(memory_space=pltpu.HBM)] * len(late) + [vmem] * 3,
        out_specs=(vmem,) * 4,
        input_output_aliases={first + i: i for i in range(3)},
        scratch_shapes=[pltpu.VMEM((BR, BA * BA), jnp.float32), pltpu.SemaphoreType.DMA],
        compiler_params=pltpu.CompilerParams(vmem_limit_bytes=SCOPED),
        name="slab",
    )(table, occ, virt, *late, *assembled)[3]


def body(
    three_center, block_dest, block_row, block_col, occ_density, virt_density, occ_mask, virt_mask
):
    owners = lax.axis_size(("ri", "pair"))
    blocks_dev = three_center.shape[0]
    ao_blocks = occ_mask.shape[1]
    width = occ_density.shape[1]
    me = lax.axis_index(("ri", "pair")).astype(jnp.int32).reshape(1)
    dest = block_dest.reshape(-1)
    outgoing, late, route = pack(me, dest, three_center, owners)
    group = ("ri", "pair")

    def exchange(slots):
        return lax.all_to_all(slots, group, split_axis=0, concat_axis=0, tiled=True)

    incoming = exchange(outgoing)
    local = jnp.concatenate(
        [
            occ_density * expand(occ_mask, BA).astype(jnp.bfloat16),
            virt_density * expand(virt_mask, BA).astype(jnp.bfloat16),
        ],
        axis=1,
    )
    need_late = jnp.broadcast_to(route[2 * owners].astype(jnp.bfloat16), (8, 2 * width))
    height = local.shape[0]
    gathered = lax.all_gather(jnp.concatenate([local, need_late], axis=0), "orb", axis=0, tiled=True)
    gathered = gathered.reshape(-1, height + 8, 2 * width)
    whole = gathered[:, :height].reshape(width, 2 * width)
    any_late = jnp.max(gathered[:, height, 0]) > 0
    table = plan(me, dest, block_row, block_col, route, owners, blocks_dev, ao_blocks)
    route, table, occ, virt, any_late = lax.optimization_barrier(
        (route, table, whole[:, :width], whole[:, width:], any_late)
    )
    incoming, late = lax.optimization_barrier((incoming, late))
    late = lax.cond(any_late, exchange, lambda slots: slots, late)
    relayed = [
        lax.ppermute(part, group, [(i, i ^ mask) for i in range(owners)])
        for part, mask in zip(forward(route, incoming), RELAY_MASKS)
    ]
    assembled = assemble(table, incoming, owners * CAP, ao_blocks)
    return slab(table, occ, virt, [*relayed, late], assembled, owners * CAP, ao_blocks)


def solution(mesh):
    placed = (
        P(("orb", "ri", "pair"), None, None),
        P("orb", None),
        P("orb"),
        P("orb"),
        P("orb", None),
        P("orb", None),
        P("orb", None),
        P("orb", None),
    )
    return jax.shard_map(
        body, mesh=mesh, in_specs=placed, out_specs=P(("orb", "ri", "pair"), None), check_vma=False
    )
```

```python
import functools

import jax
import jax.numpy as jnp
from jax import lax
from jax.experimental import pallas as pl
from jax.experimental.pallas import tpu as pltpu
from jax.sharding import PartitionSpec as P

BR = 64
BA = 32
CAP = 2
LANES = 128
PITCH = BR + 1
OWNER_BITS = 5
RELAY_SPAN_BITS = 6
RELAY_SPAN = 1 << RELAY_SPAN_BITS
RELAY_MASKS = (4, 1, 3, 8, 24)
RELAY_CAPS = (12, 2, 2, 2, 2)
NEAR_SHIFT = 4
NEAR_LOW = 0x0F0F0F0F
PLACE_BITS = 7
GROUP_BITS = 2
SCOPED = 12 * 1024 * 1024


def expand(mask_blocks, block_width):
    return jnp.repeat(jnp.repeat(mask_blocks, block_width, axis=0), block_width, axis=1)


def relay_offsets():
    offsets, total = [], 0
    for cap in RELAY_CAPS:
        offsets.append(total)
        total += cap
    return offsets, total


def groups_of(ao_blocks):
    return ao_blocks * ao_blocks >> GROUP_BITS


def bit_of(word, index):
    return lax.shift_right_logical(word, index) & 1


def pack_kernel(
    owners, blocks_dev, me_ref, dest_ref, source_ref, out_ref, late_ref, route_ref,
    named_ref, direct_ref, second_ref, used_ref, place_ref, rank_ref, kept_ref, blocks_ref, load_sem, sem,
):
    load = pltpu.make_async_copy(source_ref, blocks_ref, load_sem)
    load.start()
    me = me_ref[0]
    offsets, relays = relay_offsets()

    def tally(s):
        bits = [lax.shift_left(jnp.int32(1), dest_ref[s * blocks_dev + k]) for k in range(blocks_dev)]
        named = functools.reduce(lax.bitwise_or, bits)
        return named, functools.reduce(lax.add, bits) - named

    def clear(o, _):
        rank_ref[o] = 0
        return 0

    lax.fori_loop(0, owners, clear, 0)
    twice = tally(me)[1]
    low = jnp.int32(NEAR_LOW)
    near_twice = lax.shift_left(twice & low, NEAR_SHIFT) | (lax.shift_right_logical(twice, NEAR_SHIFT) & low)

    def send_early(k, _):
        owner = dest_ref[me * blocks_dev + k]
        rank = rank_ref[owner]
        rank_ref[owner] = rank + 1
        early = (rank == 0) & (bit_of(near_twice, owner) == 0)
        kept_ref[k] = jnp.where(early, -1, rank)

        @pl.when(early)
        def _():
            pltpu.make_async_copy(blocks_ref.at[k], out_ref.at[owner], sem).start()

        return 0

    def list_seconds(s, total):
        seen = jnp.int32(0)
        for k in range(blocks_dev):
            owner = dest_ref[s * blocks_dev + k]
            second_ref[total] = s * owners + owner
            total = total + bit_of(seen, owner)
            seen = seen | lax.shift_left(jnp.int32(1), owner)
        return total

    def start(s, total):
        named, doubled = tally(s)
        total = lax.cond(doubled != 0, lambda: list_seconds(s, total), lambda: total)
        named_ref[s] = named
        direct_ref[s] = named
        route_ref[s] = s
        route_ref[owners + s] = owners + relays + s
        place_ref[s] = s
        for m in range(len(RELAY_MASKS)):
            used_ref[m * owners + s] = 0
        return total

    seconds = lax.fori_loop(0, owners, start, jnp.int32(0))
    load.wait()
    lax.fori_loop(0, blocks_dev, send_early, 0)
    head = 2 * owners
    route_ref[head + 1] = 0

    def record(s, via, owner, rank, mask_index, place):
        @pl.when(owner == me)
        def _():
            route_ref[rank * owners + s] = owners + place

        @pl.when(via == me)
        def _():
            count = route_ref[head + 1]
            route_ref[head + 2 + count] = s * RELAY_SPAN + place
            route_ref[head + 1] = count + 1

        @pl.when(s == me)
        def _():
            place_ref[rank * owners + owner] = via

    def room(mask_index, owner):
        return used_ref[mask_index * owners + owner] < RELAY_CAPS[mask_index]

    def route(e, failed):
        pair = second_ref[e]
        s, owner = lax.shift_right_logical(pair, OWNER_BITS), pair & (owners - 1)
        named = named_ref[s]
        near = owner ^ RELAY_MASKS[0]
        core_room = room(0, owner)
        choices = [(bit_of(named, near) == 0) & core_room]
        for m in range(1, len(RELAY_MASKS)):
            choices.append((bit_of(named, owner ^ RELAY_MASKS[m]) == 0) & room(m, owner))
        swap = core_room & (bit_of(direct_ref[s], near) == 1)
        for m in range(1, len(RELAY_MASKS)):
            choices.append(swap & (bit_of(named, near ^ RELAY_MASKS[m]) == 0) & room(m, near))
        choice = jnp.int32(len(choices))
        for c in reversed(range(len(choices))):
            choice = jnp.where(choices[c], jnp.int32(c), choice)
        for c in range(len(choices)):
            m = c if c < len(RELAY_MASKS) else c - len(RELAY_MASKS) + 1

            @pl.when(choice == c)
            def _():
                target = owner if c < len(RELAY_MASKS) else near
                via = target ^ RELAY_MASKS[m]
                count = used_ref[m * owners + target]
                used_ref[m * owners + target] = count + 1
                named_ref[s] = named | lax.shift_left(jnp.int32(1), via)
                record(s, via, target, 1 if c < len(RELAY_MASKS) else 0, m, offsets[m] + count)
                if c >= len(RELAY_MASKS):
                    direct_ref[s] = direct_ref[s] ^ lax.shift_left(jnp.int32(1), near)
                    count = used_ref[owner]
                    used_ref[owner] = count + 1
                    record(s, near, owner, 1, 0, offsets[0] + count)

        return failed | (choice == len(choices)).astype(jnp.int32)

    failed = lax.fori_loop(0, seconds, route, jnp.int32(0))
    route_ref[head] = failed

    @pl.when(failed == 1)
    def _():
        def undo(s, _):
            route_ref[s] = s
            route_ref[owners + s] = owners + relays + s
            place_ref[s] = s
            return 0

        lax.fori_loop(0, owners, undo, 0)
        route_ref[head + 1] = 0

    def send(k, _):
        rank = kept_ref[k]

        @pl.when(rank >= 0)
        def _():
            owner = dest_ref[me * blocks_dev + k]
            late = (rank == 1) & (failed == 1)

            @pl.when(late)
            def _():
                pltpu.make_async_copy(blocks_ref.at[k], late_ref.at[owner], sem).start()

            @pl.when(jnp.logical_not(late))
            def _():
                slot = place_ref[rank * owners + owner]
                pltpu.make_async_copy(blocks_ref.at[k], out_ref.at[slot], sem).start()

        return 0

    lax.fori_loop(0, blocks_dev, send, 0)
    pltpu.make_async_copy(blocks_ref, out_ref.at[pl.ds(0, blocks_dev)], sem).wait()


def pack(me, dest, blocks, owners):
    blocks_dev = blocks.shape[0]
    smem = pl.BlockSpec(memory_space=pltpu.SMEM)
    hbm = pl.BlockSpec(memory_space=pl.ANY)
    slots = jax.ShapeDtypeStruct((owners,) + blocks.shape[1:], blocks.dtype)
    relays = relay_offsets()[1]
    return pl.pallas_call(
        functools.partial(pack_kernel, owners, blocks_dev),
        out_shape=(slots, slots, jax.ShapeDtypeStruct((2 * owners + 2 + relays,), jnp.int32)),
        in_specs=[smem, smem, hbm],
        out_specs=(hbm, hbm, smem),
        scratch_shapes=[
            pltpu.SMEM((owners,), jnp.int32),
            pltpu.SMEM((owners,), jnp.int32),
            pltpu.SMEM((owners * blocks_dev,), jnp.int32),
            pltpu.SMEM((len(RELAY_MASKS) * owners,), jnp.int32),
            pltpu.SMEM((2 * owners,), jnp.int32),
            pltpu.SMEM((owners,), jnp.int32),
            pltpu.SMEM((blocks_dev,), jnp.int32),
            pltpu.VMEM(blocks.shape, blocks.dtype),
            pltpu.SemaphoreType.DMA,
            pltpu.SemaphoreType.DMA,
        ],
        name="pack",
    )(me, dest, blocks)


def forward_kernel(owners, route_ref, recv_ref, *refs):
    relay_refs = refs[: len(RELAY_MASKS)]
    stage_ref, take_sem, sem = refs[-3:]
    offsets, relays = relay_offsets()
    head = 2 * owners
    count = route_ref[head + 1]

    def take(i, _):
        slot = lax.shift_right_logical(route_ref[head + 2 + i], RELAY_SPAN_BITS)
        pltpu.make_async_copy(recv_ref.at[slot], stage_ref.at[i], take_sem.at[i]).start()
        return 0

    def give(i, _):
        place = route_ref[head + 2 + i] & (RELAY_SPAN - 1)
        pltpu.make_async_copy(recv_ref.at[0], stage_ref.at[i], take_sem.at[i]).wait()
        for ref, offset, cap in zip(relay_refs, offsets, RELAY_CAPS):
            @pl.when((place >= offset) & (place < offset + cap))
            def _():
                pltpu.make_async_copy(stage_ref.at[i], ref.at[place - offset], sem).start()

        return 0

    def wait(i, _):
        pltpu.make_async_copy(stage_ref.at[0], relay_refs[0].at[0], sem).wait()
        return 0

    lax.fori_loop(0, count, take, 0)
    lax.fori_loop(0, count, give, 0)
    lax.fori_loop(0, count, wait, 0)


def forward(route, recv):
    owners = recv.shape[0]
    hbm = pl.BlockSpec(memory_space=pl.ANY)
    block = recv.shape[1:]
    return pl.pallas_call(
        functools.partial(forward_kernel, owners),
        out_shape=tuple(jax.ShapeDtypeStruct((cap,) + block, recv.dtype) for cap in RELAY_CAPS),
        in_specs=[pl.BlockSpec(memory_space=pltpu.SMEM), hbm],
        out_specs=(hbm,) * len(RELAY_CAPS),
        scratch_shapes=[
            pltpu.VMEM((relay_offsets()[1],) + block, recv.dtype),
            pltpu.SemaphoreType.DMA((relay_offsets()[1],)),
            pltpu.SemaphoreType.DMA,
        ],
        name="forward",
    )(route, recv)


def plan_kernel(
    owners, blocks_dev, ao_blocks, me_ref, dest_ref, row_ref, col_ref, route_ref, table_ref, mine_ref
):
    me = me_ref[0]
    most = owners * CAP
    cells = ao_blocks * ao_blocks

    def clear(c, _):
        table_ref[c] = most
        return 0

    lax.fori_loop(0, cells, clear, 0)
    tail = cells + 2 * most + 1
    for r in range(ao_blocks + groups_of(ao_blocks)):
        table_ref[tail + r] = 0

    def scan(s, total):
        for k in range(blocks_dev):
            index = s * blocks_dev + k
            mine_ref[total] = index
            total = total + (dest_ref[index] == me).astype(jnp.int32)
        return total

    count = lax.fori_loop(0, owners, scan, jnp.int32(0))
    table_ref[cells + 2 * most] = count

    def enter(i, before):
        index = mine_ref[i]
        s = lax.div(index, blocks_dev)
        row = row_ref[index]
        cell = row * ao_blocks + col_ref[index]
        table_ref[cells + i] = table_ref[cell]
        table_ref[cell] = i
        place = route_ref[jnp.where(s == before, owners, 0) + s]
        table_ref[cells + most + i] = place | lax.shift_left(lax.shift_right_logical(cell, GROUP_BITS), PLACE_BITS)
        late = (place >= owners).astype(jnp.int32)
        table_ref[tail + row] += 1 - late
        table_ref[tail + ao_blocks + lax.shift_right_logical(cell, GROUP_BITS)] += late
        return s

    lax.fori_loop(0, count, enter, jnp.int32(-1))


def plan(me, dest, row, col, route, owners, blocks_dev, ao_blocks):
    smem = pl.BlockSpec(memory_space=pltpu.SMEM)
    most = owners * CAP
    return pl.pallas_call(
        functools.partial(plan_kernel, owners, blocks_dev, ao_blocks),
        out_shape=jax.ShapeDtypeStruct((ao_blocks * ao_blocks + 2 * most + 1 + ao_blocks + groups_of(ao_blocks),), jnp.int32),
        in_specs=[smem] * 5,
        out_specs=smem,
        scratch_shapes=[pltpu.SMEM((most + 1,), jnp.int32)],
        name="plan",
    )(me, dest, row, col, route)


def merge_cells(most, ao_blocks, first_cell, table_ref, held, total):
    cells = ao_blocks * ao_blocks

    def merge(c, _):
        first = table_ref[c]

        @pl.when(first < most)
        def _():
            second = table_ref[cells + first]

            @pl.when(second < most)
            def _():
                total[...] = held[first].astype(jnp.float32)

                def add(slot):
                    total[...] += held[slot].astype(jnp.float32)
                    return table_ref[cells + slot]

                lax.while_loop(lambda slot: slot < most, add, second)
                held[first] = total[...].astype(held.dtype)

        return 0

    lax.fori_loop(first_cell, first_cell + (1 << GROUP_BITS), merge, 0)


def pair_shuffle():
    lane, to = (lax.broadcasted_iota(jnp.int32, (2 * LANES, 2 * LANES), axis) for axis in (0, 1))
    target = ((lane & 32) << 2) | (lane & 64) | ((lane & 128) >> 2) | (lane & 31)
    return (to == target).astype(jnp.float32).astype(jnp.bfloat16)


def place_group(first_cell, r, tile, lanes, table_ref, shuffle, held, dense, work):
    high = BA // 4
    x = []
    for j in range(4):
        s = table_ref[first_cell + j]
        x.append(jnp.concatenate([held[s, :, hi * LANES : (hi + 1) * LANES] for hi in range(high)], axis=0))
    low = lax.broadcasted_iota(jnp.int32, x[0].shape, 1) < LANES // 2
    z = [None] * 4
    for a in (0, 1):
        z[a] = jnp.where(low, x[a], pltpu.roll(x[a + 2], LANES // 2, 1))
        z[a + 2] = jnp.where(low, pltpu.roll(x[a], LANES // 2, 1), x[a + 2])
    y = [
        jnp.dot(jnp.concatenate(z[a : a + 2], axis=1), shuffle, preferred_element_type=jnp.float32)
        for a in (0, 2)
    ]
    for hi in range(high):
        for j in range(4):
            mu = r * BA + hi * 4 + j
            part = y[j // 2][hi * BR : (hi + 1) * BR, (j % 2) * LANES : (j % 2 + 1) * LANES]
            work[tile, pl.ds(mu * PITCH, BR), :] = part
            dense[mu, :, lanes] = part.astype(jnp.bfloat16)


def assemble_kernel(most, ao_blocks, table_ref, recv_ref, held, dense, work, total, sem):
    cells = ao_blocks * ao_blocks
    per_tile = LANES // BA
    tiles = ao_blocks // per_tile
    tail = cells + 2 * most + 1

    def fetch(i, _):
        entry = table_ref[cells + most + i]
        place = entry & ((1 << PLACE_BITS) - 1)
        row = lax.div(lax.shift_right_logical(entry, PLACE_BITS), tiles)

        @pl.when(place < recv_ref.shape[0])
        def _():
            pltpu.make_async_copy(recv_ref.at[place], held.at[i], sem.at[row]).start()

        return 0

    lax.fori_loop(0, table_ref[cells + 2 * most], fetch, 0)
    held[most] = jnp.zeros(held.shape[1:], held.dtype)
    shuffle = pair_shuffle()

    def row(r, _):
        def arrive(i, _):
            pltpu.make_async_copy(recv_ref.at[0], held.at[0], sem.at[r]).wait()
            return 0

        lax.fori_loop(0, table_ref[tail + r], arrive, 0)
        for tile in range(tiles):
            first_cell = r * ao_blocks + tile * per_tile

            @pl.when(table_ref[tail + ao_blocks + r * tiles + tile] == 0)
            def _():
                merge_cells(most, ao_blocks, first_cell, table_ref, held, total)
                lanes = slice(tile * LANES, (tile + 1) * LANES)
                place_group(first_cell, r, tile, lanes, table_ref, shuffle, held, dense, work)

        return 0

    lax.fori_loop(0, ao_blocks, row, 0)


def assemble(table, recv, most, ao_blocks):
    width = ao_blocks * BA
    vmem = pl.BlockSpec(memory_space=pltpu.VMEM)
    return pl.pallas_call(
        functools.partial(assemble_kernel, most, ao_blocks),
        out_shape=(
            pltpu.VMEM((most + 1, BR, BA * BA), jnp.bfloat16),
            pltpu.VMEM((width, BR, width), jnp.bfloat16),
            pltpu.VMEM((width // LANES, width * PITCH, LANES), jnp.float32),
        ),
        in_specs=[pl.BlockSpec(memory_space=pltpu.SMEM), pl.BlockSpec(memory_space=pl.ANY)],
        out_specs=(vmem, vmem, vmem),
        scratch_shapes=[pltpu.VMEM((BR, BA * BA), jnp.float32), pltpu.SemaphoreType.DMA((ao_blocks,))],
        compiler_params=pltpu.CompilerParams(vmem_limit_bytes=SCOPED),
        cost_estimate=pl.CostEstimate(flops=1 << 32, bytes_accessed=1 << 24, transcendentals=0),
        name="assemble",
    )(table, recv)


def slab_kernel(most, ao_blocks, table_ref, occ_ref, virt_ref, *refs):
    late_refs = refs[:-9]
    held, dense, work = refs[-6:-3]
    out_ref, total, sem = refs[-3:]
    width = ao_blocks * BA
    cells = ao_blocks * ao_blocks
    per_tile = LANES // BA
    tiles = width // LANES
    tail = cells + 2 * most + 1
    slots = most // CAP

    def fetch(i, _):
        entry = table_ref[cells + most + i]
        place = entry & ((1 << PLACE_BITS) - 1)
        group = lax.shift_right_logical(entry, PLACE_BITS)

        @pl.when(place >= slots)
        def _():
            offset = slots
            for ref in late_refs:
                @pl.when((place >= offset) & (place < offset + ref.shape[0]))
                def _():
                    pltpu.make_async_copy(ref.at[place - offset], held.at[i], sem.at[group]).start()

                offset += ref.shape[0]

        return 0

    lax.fori_loop(0, table_ref[cells + 2 * most], fetch, 0)
    occ_t = occ_ref[...].astype(jnp.float32).T.astype(jnp.bfloat16)
    shuffle = pair_shuffle()

    def place(step, _):
        late = table_ref[tail + ao_blocks + step]

        @pl.when(late > 0)
        def _():
            def arrive(i, _):
                pltpu.make_async_copy(late_refs[0].at[0], held.at[0], sem.at[step]).wait()
                return 0

            lax.fori_loop(0, late, arrive, 0)
            r, tile = step // tiles, step % tiles
            first_cell = step * per_tile
            merge_cells(most, ao_blocks, first_cell, table_ref, held, total)
            lanes = pl.ds(pl.multiple_of(tile * LANES, LANES), LANES)
            place_group(first_cell, r, tile, lanes, table_ref, shuffle, held, dense, work)

        return 0

    lax.fori_loop(0, groups_of(ao_blocks), place, 0)

    virt = virt_ref[...]

    def transform(i, _):
        for j in range(16):
            rows = pl.ds(i * 16 + j, width, stride=PITCH)
            part = jnp.concatenate([work[t, rows, :] for t in range(tiles)], axis=1).astype(jnp.bfloat16)
            half = jnp.dot(occ_t, part, preferred_element_type=jnp.float32).astype(jnp.bfloat16)
            both = jnp.dot(half, virt, preferred_element_type=jnp.float32)
            for t in range(tiles):
                work[t, rows, :] = both[:, t * LANES : (t + 1) * LANES]
        return 0

    lax.fori_loop(0, BR // 16, transform, 0)

    def contract(i, acc):
        left, right = [], []
        for j in range(32):
            mu = i * 32 + j
            left += [work[t, pl.ds(mu * PITCH, BR), :] for t in range(tiles)]
            right.append(dense[mu])
        return acc + lax.dot_general(
            jnp.concatenate(left, axis=1).astype(jnp.bfloat16),
            jnp.concatenate(right, axis=1),
            (((1,), (1,)), ((), ())),
            preferred_element_type=jnp.float32,
        )

    out_ref[...] = lax.fori_loop(0, width // 32, contract, jnp.zeros((BR, BR), jnp.float32))


def slab(table, occ, virt, late, assembled, most, ao_blocks):
    smem = pl.BlockSpec(memory_space=pltpu.SMEM)
    vmem = pl.BlockSpec(memory_space=pltpu.VMEM)
    first = 3 + len(late)
    return pl.pallas_call(
        functools.partial(slab_kernel, most, ao_blocks),
        out_shape=tuple(pltpu.VMEM(a.shape, a.dtype) for a in assembled)
        + (jax.ShapeDtypeStruct((BR, BR), jnp.float32),),
        in_specs=[smem, vmem, vmem] + [pl.BlockSpec(memory_space=pltpu.HBM)] * len(late) + [vmem] * 3,
        out_specs=(vmem,) * 4,
        input_output_aliases={first + i: i for i in range(3)},
        scratch_shapes=[
            pltpu.VMEM((BR, BA * BA), jnp.float32),
            pltpu.SemaphoreType.DMA((groups_of(ao_blocks),)),
        ],
        compiler_params=pltpu.CompilerParams(vmem_limit_bytes=SCOPED),
        name="slab",
    )(table, occ, virt, *late, *assembled)[3]


def body(
    three_center, block_dest, block_row, block_col, occ_density, virt_density, occ_mask, virt_mask
):
    owners = lax.axis_size(("ri", "pair"))
    blocks_dev = three_center.shape[0]
    ao_blocks = occ_mask.shape[1]
    width = occ_density.shape[1]
    me = lax.axis_index(("ri", "pair")).astype(jnp.int32).reshape(1)
    dest = block_dest.reshape(-1)
    outgoing, late, route = pack(me, dest, three_center, owners)
    group = ("ri", "pair")

    def exchange(slots):
        return lax.all_to_all(slots, group, split_axis=0, concat_axis=0, tiled=True)

    incoming = exchange(outgoing)
    local = jnp.concatenate(
        [
            occ_density * expand(occ_mask, BA).astype(jnp.bfloat16),
            virt_density * expand(virt_mask, BA).astype(jnp.bfloat16),
        ],
        axis=1,
    )
    need_late = jnp.broadcast_to(route[2 * owners].astype(jnp.bfloat16), (8, 2 * width))
    height = local.shape[0]
    gathered = lax.all_gather(jnp.concatenate([local, need_late], axis=0), "orb", axis=0, tiled=True)
    gathered = gathered.reshape(-1, height + 8, 2 * width)
    whole = gathered[:, :height].reshape(width, 2 * width)
    any_late = jnp.max(gathered[:, height, 0]) > 0
    table = plan(me, dest, block_row, block_col, route, owners, blocks_dev, ao_blocks)
    route, table, occ, virt, any_late = lax.optimization_barrier(
        (route, table, whole[:, :width], whole[:, width:], any_late)
    )
    incoming, late = lax.optimization_barrier((incoming, late))
    late = lax.cond(any_late, exchange, lambda slots: slots, late)
    relayed = [
        lax.ppermute(part, group, [(i, i ^ mask) for i in range(owners)])
        for part, mask in zip(forward(route, incoming), RELAY_MASKS)
    ]
    assembled = assemble(table, incoming, owners * CAP, ao_blocks)
    return slab(table, occ, virt, [*relayed, late], assembled, owners * CAP, ao_blocks)


def solution(mesh):
    placed = (
        P(("orb", "ri", "pair"), None, None),
        P("orb", None),
        P("orb"),
        P("orb"),
        P("orb", None),
        P("orb", None),
        P("orb", None),
        P("orb", None),
    )
    return jax.shard_map(
        body, mesh=mesh, in_specs=placed, out_specs=P(("orb", "ri", "pair"), None), check_vma=False
    )
```

```python
import functools

import jax
import jax.numpy as jnp
from jax import lax
from jax.experimental import pallas as pl
from jax.experimental.pallas import tpu as pltpu
from jax.sharding import PartitionSpec as P

BR = 64
BA = 32
CAP = 2
LANES = 128
PITCH = BR + 1
OWNER_BITS = 5
RELAY_SPAN_BITS = 6
RELAY_SPAN = 1 << RELAY_SPAN_BITS
RELAY_MASKS = (4, 1, 3, 8, 24)
RELAY_CAPS = (12, 2, 2, 2, 2)
NEAR_SHIFT = 4
NEAR_LOW = 0x0F0F0F0F
PLACE_BITS = 7
GROUP_BITS = 2
SCOPED = 12 * 1024 * 1024


def expand(mask_blocks, block_width):
    return jnp.repeat(jnp.repeat(mask_blocks, block_width, axis=0), block_width, axis=1)


def relay_offsets():
    offsets, total = [], 0
    for cap in RELAY_CAPS:
        offsets.append(total)
        total += cap
    return offsets, total


def groups_of(ao_blocks):
    return ao_blocks * ao_blocks >> GROUP_BITS


def bit_of(word, index):
    return lax.shift_right_logical(word, index) & 1


def pack_kernel(
    owners, blocks_dev, me_ref, dest_ref, source_ref, out_ref, late_ref, route_ref,
    named_ref, direct_ref, second_ref, used_ref, place_ref, rank_ref, kept_ref, blocks_ref, load_sem, sem,
):
    load = pltpu.make_async_copy(source_ref, blocks_ref, load_sem)
    load.start()
    me = me_ref[0]
    offsets, relays = relay_offsets()

    def tally(s):
        bits = [lax.shift_left(jnp.int32(1), dest_ref[s * blocks_dev + k]) for k in range(blocks_dev)]
        named = functools.reduce(lax.bitwise_or, bits)
        return named, functools.reduce(lax.add, bits) - named

    def clear(o, _):
        rank_ref[o] = 0
        return 0

    lax.fori_loop(0, owners, clear, 0)
    twice = tally(me)[1]
    low = jnp.int32(NEAR_LOW)
    near_twice = lax.shift_left(twice & low, NEAR_SHIFT) | (lax.shift_right_logical(twice, NEAR_SHIFT) & low)

    def send_early(k, _):
        owner = dest_ref[me * blocks_dev + k]
        rank = rank_ref[owner]
        rank_ref[owner] = rank + 1
        early = (rank == 0) & (bit_of(near_twice, owner) == 0)
        kept_ref[k] = jnp.where(early, -1, rank)

        @pl.when(early)
        def _():
            pltpu.make_async_copy(blocks_ref.at[k], out_ref.at[owner], sem).start()

        return 0

    def list_seconds(s, total):
        seen = jnp.int32(0)
        for k in range(blocks_dev):
            owner = dest_ref[s * blocks_dev + k]
            second_ref[total] = s * owners + owner
            total = total + bit_of(seen, owner)
            seen = seen | lax.shift_left(jnp.int32(1), owner)
        return total

    def start(s, total):
        named, doubled = tally(s)
        total = lax.cond(doubled != 0, lambda: list_seconds(s, total), lambda: total)
        named_ref[s] = named
        direct_ref[s] = named
        route_ref[s] = s
        route_ref[owners + s] = owners + relays + s
        place_ref[s] = s
        for m in range(len(RELAY_MASKS)):
            used_ref[m * owners + s] = 0
        return total

    seconds = lax.fori_loop(0, owners, start, jnp.int32(0))
    load.wait()
    lax.fori_loop(0, blocks_dev, send_early, 0)
    head = 2 * owners
    route_ref[head + 1] = 0

    def record(s, via, owner, rank, place):
        @pl.when(owner == me)
        def _():
            route_ref[rank * owners + s] = owners + place

        @pl.when(via == me)
        def _():
            count = route_ref[head + 1]
            route_ref[head + 2 + count] = s * RELAY_SPAN + place
            route_ref[head + 1] = count + 1

        @pl.when(s == me)
        def _():
            place_ref[rank * owners + owner] = via

    def room(mask_index, owner):
        return used_ref[mask_index * owners + owner] < RELAY_CAPS[mask_index]

    def route(e, failed):
        pair = second_ref[e]
        s, owner = lax.shift_right_logical(pair, OWNER_BITS), pair & (owners - 1)
        named = named_ref[s]
        near = owner ^ RELAY_MASKS[0]
        core_room = room(0, owner)
        choices = [(bit_of(named, near) == 0) & core_room]
        for m in range(1, len(RELAY_MASKS)):
            choices.append((bit_of(named, owner ^ RELAY_MASKS[m]) == 0) & room(m, owner))
        swap = core_room & (bit_of(direct_ref[s], near) == 1)
        for m in range(1, len(RELAY_MASKS)):
            choices.append(swap & (bit_of(named, near ^ RELAY_MASKS[m]) == 0) & room(m, near))
        choice = jnp.int32(len(choices))
        for c in reversed(range(len(choices))):
            choice = jnp.where(choices[c], jnp.int32(c), choice)
        swapped = choice >= len(RELAY_MASKS)
        m = jnp.where(swapped, choice - len(RELAY_MASKS) + 1, choice)
        mask, offset = jnp.int32(RELAY_MASKS[0]), jnp.int32(offsets[0])
        for i in range(1, len(RELAY_MASKS)):
            mask = jnp.where(m == i, RELAY_MASKS[i], mask)
            offset = jnp.where(m == i, offsets[i], offset)
        target = jnp.where(swapped, near, owner)
        via = target ^ mask

        @pl.when(choice < len(choices))
        def _():
            count = used_ref[m * owners + target]
            used_ref[m * owners + target] = count + 1
            named_ref[s] = named | lax.shift_left(jnp.int32(1), via)
            record(s, via, target, jnp.where(swapped, 0, 1), offset + count)

            @pl.when(swapped)
            def _():
                direct_ref[s] = direct_ref[s] ^ lax.shift_left(jnp.int32(1), near)
                count = used_ref[owner]
                used_ref[owner] = count + 1
                record(s, near, owner, 1, offsets[0] + count)

        return failed | (choice == len(choices)).astype(jnp.int32)

    failed = lax.fori_loop(0, seconds, route, jnp.int32(0))
    route_ref[head] = failed

    @pl.when(failed == 1)
    def _():
        def undo(s, _):
            route_ref[s] = s
            route_ref[owners + s] = owners + relays + s
            place_ref[s] = s
            return 0

        lax.fori_loop(0, owners, undo, 0)
        route_ref[head + 1] = 0

    def send(k, _):
        rank = kept_ref[k]

        @pl.when(rank >= 0)
        def _():
            owner = dest_ref[me * blocks_dev + k]
            late = (rank == 1) & (failed == 1)

            @pl.when(late)
            def _():
                pltpu.make_async_copy(blocks_ref.at[k], late_ref.at[owner], sem).start()

            @pl.when(jnp.logical_not(late))
            def _():
                slot = place_ref[rank * owners + owner]
                pltpu.make_async_copy(blocks_ref.at[k], out_ref.at[slot], sem).start()

        return 0

    lax.fori_loop(0, blocks_dev, send, 0)
    pltpu.make_async_copy(blocks_ref, out_ref.at[pl.ds(0, blocks_dev)], sem).wait()


def pack(me, dest, blocks, owners):
    blocks_dev = blocks.shape[0]
    smem = pl.BlockSpec(memory_space=pltpu.SMEM)
    hbm = pl.BlockSpec(memory_space=pl.ANY)
    slots = jax.ShapeDtypeStruct((owners,) + blocks.shape[1:], blocks.dtype)
    relays = relay_offsets()[1]
    return pl.pallas_call(
        functools.partial(pack_kernel, owners, blocks_dev),
        out_shape=(slots, slots, jax.ShapeDtypeStruct((2 * owners + 2 + relays,), jnp.int32)),
        in_specs=[smem, smem, hbm],
        out_specs=(hbm, hbm, smem),
        scratch_shapes=[
            pltpu.SMEM((owners,), jnp.int32),
            pltpu.SMEM((owners,), jnp.int32),
            pltpu.SMEM((owners * blocks_dev,), jnp.int32),
            pltpu.SMEM((len(RELAY_MASKS) * owners,), jnp.int32),
            pltpu.SMEM((2 * owners,), jnp.int32),
            pltpu.SMEM((owners,), jnp.int32),
            pltpu.SMEM((blocks_dev,), jnp.int32),
            pltpu.VMEM(blocks.shape, blocks.dtype),
            pltpu.SemaphoreType.DMA,
            pltpu.SemaphoreType.DMA,
        ],
        name="pack",
    )(me, dest, blocks)


def forward_kernel(owners, route_ref, recv_ref, *refs):
    relay_refs = refs[: len(RELAY_MASKS)]
    stage_ref, take_sem, sem = refs[-3:]
    offsets, relays = relay_offsets()
    head = 2 * owners
    count = route_ref[head + 1]

    def take(i, _):
        slot = lax.shift_right_logical(route_ref[head + 2 + i], RELAY_SPAN_BITS)
        pltpu.make_async_copy(recv_ref.at[slot], stage_ref.at[i], take_sem.at[i]).start()
        return 0

    def give(i, _):
        place = route_ref[head + 2 + i] & (RELAY_SPAN - 1)
        pltpu.make_async_copy(recv_ref.at[0], stage_ref.at[i], take_sem.at[i]).wait()
        for ref, offset, cap in zip(relay_refs, offsets, RELAY_CAPS):
            @pl.when((place >= offset) & (place < offset + cap))
            def _():
                pltpu.make_async_copy(stage_ref.at[i], ref.at[place - offset], sem).start()

        return 0

    def wait(i, _):
        pltpu.make_async_copy(stage_ref.at[0], relay_refs[0].at[0], sem).wait()
        return 0

    lax.fori_loop(0, count, take, 0)
    lax.fori_loop(0, count, give, 0)
    lax.fori_loop(0, count, wait, 0)


def forward(route, recv):
    owners = recv.shape[0]
    hbm = pl.BlockSpec(memory_space=pl.ANY)
    block = recv.shape[1:]
    return pl.pallas_call(
        functools.partial(forward_kernel, owners),
        out_shape=tuple(jax.ShapeDtypeStruct((cap,) + block, recv.dtype) for cap in RELAY_CAPS),
        in_specs=[pl.BlockSpec(memory_space=pltpu.SMEM), hbm],
        out_specs=(hbm,) * len(RELAY_CAPS),
        scratch_shapes=[
            pltpu.VMEM((relay_offsets()[1],) + block, recv.dtype),
            pltpu.SemaphoreType.DMA((relay_offsets()[1],)),
            pltpu.SemaphoreType.DMA,
        ],
        name="forward",
    )(route, recv)


def plan_kernel(
    owners, blocks_dev, ao_blocks, me_ref, dest_ref, row_ref, col_ref, route_ref, table_ref, mine_ref
):
    me = me_ref[0]
    most = owners * CAP
    cells = ao_blocks * ao_blocks

    def clear(c, _):
        table_ref[c] = most
        return 0

    lax.fori_loop(0, cells, clear, 0)
    tail = cells + 2 * most + 1
    for r in range(ao_blocks + groups_of(ao_blocks)):
        table_ref[tail + r] = 0

    def scan(s, total):
        for k in range(blocks_dev):
            index = s * blocks_dev + k
            mine_ref[total] = index
            total = total + (dest_ref[index] == me).astype(jnp.int32)
        return total

    count = lax.fori_loop(0, owners, scan, jnp.int32(0))
    table_ref[cells + 2 * most] = count

    def enter(i, before):
        index = mine_ref[i]
        s = lax.div(index, blocks_dev)
        row = row_ref[index]
        cell = row * ao_blocks + col_ref[index]
        table_ref[cells + i] = table_ref[cell]
        table_ref[cell] = i
        place = route_ref[jnp.where(s == before, owners, 0) + s]
        table_ref[cells + most + i] = place | lax.shift_left(lax.shift_right_logical(cell, GROUP_BITS), PLACE_BITS)
        late = (place >= owners).astype(jnp.int32)
        table_ref[tail + row] += 1 - late
        table_ref[tail + ao_blocks + lax.shift_right_logical(cell, GROUP_BITS)] += late
        return s

    lax.fori_loop(0, count, enter, jnp.int32(-1))


def plan(me, dest, row, col, route, owners, blocks_dev, ao_blocks):
    smem = pl.BlockSpec(memory_space=pltpu.SMEM)
    most = owners * CAP
    return pl.pallas_call(
        functools.partial(plan_kernel, owners, blocks_dev, ao_blocks),
        out_shape=jax.ShapeDtypeStruct((ao_blocks * ao_blocks + 2 * most + 1 + ao_blocks + groups_of(ao_blocks),), jnp.int32),
        in_specs=[smem] * 5,
        out_specs=smem,
        scratch_shapes=[pltpu.SMEM((most + 1,), jnp.int32)],
        name="plan",
    )(me, dest, row, col, route)


def merge_cells(most, ao_blocks, first_cell, table_ref, held, total):
    cells = ao_blocks * ao_blocks

    def merge(c, _):
        first = table_ref[c]

        @pl.when(first < most)
        def _():
            second = table_ref[cells + first]

            @pl.when(second < most)
            def _():
                total[...] = held[first].astype(jnp.float32)

                def add(slot):
                    total[...] += held[slot].astype(jnp.float32)
                    return table_ref[cells + slot]

                lax.while_loop(lambda slot: slot < most, add, second)
                held[first] = total[...].astype(held.dtype)

        return 0

    lax.fori_loop(first_cell, first_cell + (1 << GROUP_BITS), merge, 0)


def pair_shuffle():
    lane, to = (lax.broadcasted_iota(jnp.int32, (2 * LANES, 2 * LANES), axis) for axis in (0, 1))
    target = ((lane & 32) << 2) | (lane & 64) | ((lane & 128) >> 2) | (lane & 31)
    return (to == target).astype(jnp.float32).astype(jnp.bfloat16)


def place_group(first_cell, r, tile, lanes, table_ref, shuffle, held, dense, work):
    high = BA // 4
    x = []
    for j in range(4):
        s = table_ref[first_cell + j]
        x.append(jnp.concatenate([held[s, :, hi * LANES : (hi + 1) * LANES] for hi in range(high)], axis=0))
    low = lax.broadcasted_iota(jnp.int32, x[0].shape, 1) < LANES // 2
    z = [None] * 4
    for a in (0, 1):
        z[a] = jnp.where(low, x[a], pltpu.roll(x[a + 2], LANES // 2, 1))
        z[a + 2] = jnp.where(low, pltpu.roll(x[a], LANES // 2, 1), x[a + 2])
    y = [
        jnp.dot(jnp.concatenate(z[a : a + 2], axis=1), shuffle, preferred_element_type=jnp.float32)
        for a in (0, 2)
    ]
    for hi in range(high):
        for j in range(4):
            mu = r * BA + hi * 4 + j
            part = y[j // 2][hi * BR : (hi + 1) * BR, (j % 2) * LANES : (j % 2 + 1) * LANES]
            work[tile, pl.ds(mu * PITCH, BR), :] = part
            dense[mu, :, lanes] = part.astype(jnp.bfloat16)


def assemble_kernel(most, ao_blocks, table_ref, recv_ref, held, dense, work, total, sem):
    cells = ao_blocks * ao_blocks
    per_tile = LANES // BA
    tiles = ao_blocks // per_tile
    tail = cells + 2 * most + 1

    def fetch(i, _):
        entry = table_ref[cells + most + i]
        place = entry & ((1 << PLACE_BITS) - 1)
        row = lax.div(lax.shift_right_logical(entry, PLACE_BITS), tiles)

        @pl.when(place < recv_ref.shape[0])
        def _():
            pltpu.make_async_copy(recv_ref.at[place], held.at[i], sem.at[row]).start()

        return 0

    lax.fori_loop(0, table_ref[cells + 2 * most], fetch, 0)
    held[most] = jnp.zeros(held.shape[1:], held.dtype)
    shuffle = pair_shuffle()

    def row(r, _):
        def arrive(i, _):
            pltpu.make_async_copy(recv_ref.at[0], held.at[0], sem.at[r]).wait()
            return 0

        lax.fori_loop(0, table_ref[tail + r], arrive, 0)
        for tile in range(tiles):
            first_cell = r * ao_blocks + tile * per_tile

            @pl.when(table_ref[tail + ao_blocks + r * tiles + tile] == 0)
            def _():
                merge_cells(most, ao_blocks, first_cell, table_ref, held, total)
                lanes = slice(tile * LANES, (tile + 1) * LANES)
                place_group(first_cell, r, tile, lanes, table_ref, shuffle, held, dense, work)

        return 0

    lax.fori_loop(0, ao_blocks, row, 0)


def assemble(table, recv, most, ao_blocks):
    width = ao_blocks * BA
    vmem = pl.BlockSpec(memory_space=pltpu.VMEM)
    return pl.pallas_call(
        functools.partial(assemble_kernel, most, ao_blocks),
        out_shape=(
            pltpu.VMEM((most + 1, BR, BA * BA), jnp.bfloat16),
            pltpu.VMEM((width, BR, width), jnp.bfloat16),
            pltpu.VMEM((width // LANES, width * PITCH, LANES), jnp.float32),
        ),
        in_specs=[pl.BlockSpec(memory_space=pltpu.SMEM), pl.BlockSpec(memory_space=pl.ANY)],
        out_specs=(vmem, vmem, vmem),
        scratch_shapes=[pltpu.VMEM((BR, BA * BA), jnp.float32), pltpu.SemaphoreType.DMA((ao_blocks,))],
        compiler_params=pltpu.CompilerParams(vmem_limit_bytes=SCOPED),
        cost_estimate=pl.CostEstimate(flops=1 << 32, bytes_accessed=1 << 24, transcendentals=0),
        name="assemble",
    )(table, recv)


def slab_kernel(most, ao_blocks, table_ref, occ_ref, virt_ref, *refs):
    late_refs = refs[:-9]
    held, dense, work = refs[-6:-3]
    out_ref, total, sem = refs[-3:]
    width = ao_blocks * BA
    cells = ao_blocks * ao_blocks
    per_tile = LANES // BA
    tiles = width // LANES
    tail = cells + 2 * most + 1
    slots = most // CAP

    def fetch(i, _):
        entry = table_ref[cells + most + i]
        place = entry & ((1 << PLACE_BITS) - 1)
        group = lax.shift_right_logical(entry, PLACE_BITS)

        @pl.when(place >= slots)
        def _():
            offset = slots
            for ref in late_refs:
                @pl.when((place >= offset) & (place < offset + ref.shape[0]))
                def _():
                    pltpu.make_async_copy(ref.at[place - offset], held.at[i], sem.at[group]).start()

                offset += ref.shape[0]

        return 0

    lax.fori_loop(0, table_ref[cells + 2 * most], fetch, 0)
    occ_t = occ_ref[...].astype(jnp.float32).T.astype(jnp.bfloat16)
    shuffle = pair_shuffle()

    def place(step, _):
        late = table_ref[tail + ao_blocks + step]

        @pl.when(late > 0)
        def _():
            def arrive(i, _):
                pltpu.make_async_copy(late_refs[0].at[0], held.at[0], sem.at[step]).wait()
                return 0

            lax.fori_loop(0, late, arrive, 0)
            r, tile = step // tiles, step % tiles
            first_cell = step * per_tile
            merge_cells(most, ao_blocks, first_cell, table_ref, held, total)
            lanes = pl.ds(pl.multiple_of(tile * LANES, LANES), LANES)
            place_group(first_cell, r, tile, lanes, table_ref, shuffle, held, dense, work)

        return 0

    lax.fori_loop(0, groups_of(ao_blocks), place, 0)

    virt = virt_ref[...]

    def transform(i, _):
        for j in range(16):
            rows = pl.ds(i * 16 + j, width, stride=PITCH)
            part = jnp.concatenate([work[t, rows, :] for t in range(tiles)], axis=1).astype(jnp.bfloat16)
            half = jnp.dot(occ_t, part, preferred_element_type=jnp.float32).astype(jnp.bfloat16)
            both = jnp.dot(half, virt, preferred_element_type=jnp.float32)
            for t in range(tiles):
                work[t, rows, :] = both[:, t * LANES : (t + 1) * LANES]
        return 0

    lax.fori_loop(0, BR // 16, transform, 0)

    def contract(i, acc):
        left, right = [], []
        for j in range(32):
            mu = i * 32 + j
            left += [work[t, pl.ds(mu * PITCH, BR), :] for t in range(tiles)]
            right.append(dense[mu])
        return acc + lax.dot_general(
            jnp.concatenate(left, axis=1).astype(jnp.bfloat16),
            jnp.concatenate(right, axis=1),
            (((1,), (1,)), ((), ())),
            preferred_element_type=jnp.float32,
        )

    out_ref[...] = lax.fori_loop(0, width // 32, contract, jnp.zeros((BR, BR), jnp.float32))


def slab(table, occ, virt, late, assembled, most, ao_blocks):
    smem = pl.BlockSpec(memory_space=pltpu.SMEM)
    vmem = pl.BlockSpec(memory_space=pltpu.VMEM)
    first = 3 + len(late)
    return pl.pallas_call(
        functools.partial(slab_kernel, most, ao_blocks),
        out_shape=tuple(pltpu.VMEM(a.shape, a.dtype) for a in assembled)
        + (jax.ShapeDtypeStruct((BR, BR), jnp.float32),),
        in_specs=[smem, vmem, vmem] + [pl.BlockSpec(memory_space=pltpu.HBM)] * len(late) + [vmem] * 3,
        out_specs=(vmem,) * 4,
        input_output_aliases={first + i: i for i in range(3)},
        scratch_shapes=[
            pltpu.VMEM((BR, BA * BA), jnp.float32),
            pltpu.SemaphoreType.DMA((groups_of(ao_blocks),)),
        ],
        compiler_params=pltpu.CompilerParams(vmem_limit_bytes=SCOPED),
        name="slab",
    )(table, occ, virt, *late, *assembled)[3]


def body(
    three_center, block_dest, block_row, block_col, occ_density, virt_density, occ_mask, virt_mask
):
    owners = lax.axis_size(("ri", "pair"))
    blocks_dev = three_center.shape[0]
    ao_blocks = occ_mask.shape[1]
    width = occ_density.shape[1]
    me = lax.axis_index(("ri", "pair")).astype(jnp.int32).reshape(1)
    dest = block_dest.reshape(-1)
    outgoing, late, route = pack(me, dest, three_center, owners)
    group = ("ri", "pair")

    def exchange(slots):
        return lax.all_to_all(slots, group, split_axis=0, concat_axis=0, tiled=True)

    incoming = exchange(outgoing)
    local = jnp.concatenate(
        [
            occ_density * expand(occ_mask, BA).astype(jnp.bfloat16),
            virt_density * expand(virt_mask, BA).astype(jnp.bfloat16),
        ],
        axis=1,
    )
    need_late = jnp.broadcast_to(route[2 * owners].astype(jnp.bfloat16), (8, 2 * width))
    height = local.shape[0]
    gathered = lax.all_gather(jnp.concatenate([local, need_late], axis=0), "orb", axis=0, tiled=True)
    gathered = gathered.reshape(-1, height + 8, 2 * width)
    whole = gathered[:, :height].reshape(width, 2 * width)
    any_late = jnp.max(gathered[:, height, 0]) > 0
    table = plan(me, dest, block_row, block_col, route, owners, blocks_dev, ao_blocks)
    route, table, occ, virt, any_late = lax.optimization_barrier(
        (route, table, whole[:, :width], whole[:, width:], any_late)
    )
    incoming, late = lax.optimization_barrier((incoming, late))
    late = lax.cond(any_late, exchange, lambda slots: slots, late)
    relayed = [
        lax.ppermute(part, group, [(i, i ^ mask) for i in range(owners)])
        for part, mask in zip(forward(route, incoming), RELAY_MASKS)
    ]
    assembled = assemble(table, incoming, owners * CAP, ao_blocks)
    return slab(table, occ, virt, [*relayed, late], assembled, owners * CAP, ao_blocks)


def solution(mesh):
    placed = (
        P(("orb", "ri", "pair"), None, None),
        P("orb", None),
        P("orb"),
        P("orb"),
        P("orb", None),
        P("orb", None),
        P("orb", None),
        P("orb", None),
    )
    return jax.shard_map(
        body, mesh=mesh, in_specs=placed, out_specs=P(("orb", "ri", "pair"), None), check_vma=False
    )
```
